256 devices in a mesh: wave: 64 (over z, y, core), field: 4 (over x).
Axes of the slice: x: 4, y: 4, z: 8, core: 2. Of those that a mesh axis runs over, the one named last changes fastest.
Arguments:
- spectra: bfloat16 [640, 2, 160, 640], P('wave', None, 'field'), may hold values from -0.15625 to 0.15625
- legendre: bfloat16 [640, 640, 640], P('wave'), may hold values from -0.25 to 0.25
- block_mask: int32 [640, 10, 10], P('wave'), may hold values from 0 to 1, as said below
- wave_slot: int32 [640], replicated, may hold values from 0 to 639, as said below
- lat_order: int32 [1280], replicated, may hold values from 0 to 1279, each once
- level_order: int32 [160], replicated, may hold values from 0 to 159, each once
Outputs:
- grid_fields: bfloat16 [1280, 160, 3072], P('wave', None, 'field')
The draws below stay inside these ranges and needn't reach their ends.
Inputs may be any that keep to these rules, and one draw needn't show every extreme that they name: `wave_slot`: each wavenumber from 0 to 639 is held by exactly one slot. `block_mask`: a block is 0 where every total wavenumber of its row block lies below the slot's wavenumber; otherwise it is 0 only in the first few latitude blocks from the pole, fewer than half of them.
All inputs are finite; a program needn't handle non-finite values.
Results may differ from the reference program's by a relative error of at most 0.009.
Values may be sent and summed in bfloat16 or wider, within the bound.
A program may use at most 128 MiB of HBM per device.

```python
import jax
import jax.numpy as jnp
from jax import lax

BLOCK = 64
NLON = 3072
TRUNC = 640
NLAT = 1280
FL = 160
NB = 10


def wave_table(key):
    return jax.random.permutation(jax.random.fold_in(key, 7), jnp.arange(TRUNC, dtype=jnp.int32))


def draw_wave_slot(key, part):
    return wave_table(key)


def draw_block_mask(key, part):
    wavenums = wave_table(key)
    most_drop = wavenums * NB // (2 * TRUNC)
    drops = jax.random.randint(jax.random.fold_in(key, 11), (TRUNC,), 0, most_drop + 1)
    blocks = jnp.arange(NB, dtype=jnp.int32)
    below = blocks[None, :, None] * BLOCK + BLOCK - 1 >= wavenums[:, None, None]
    polar = blocks[None, None, :] >= drops[:, None, None]
    return (below & polar).astype(jnp.int32)


def shard_levels(key, extent, pieces, low, largest):
    factor_of = 1.0
    for dim, shards_of in pieces:
        steps = jax.random.uniform(jax.random.fold_in(jax.random.fold_in(key, 6), dim), (shards_of,), jnp.float32, low / len(pieces), largest / len(pieces))
        factor_of = factor_of * jnp.repeat(jnp.exp(steps), extent[dim] // shards_of).reshape((-1,) + (1,) * (len(extent) - 1 - dim))
    return factor_of


def centred(stream_key, shape, spread, most, pieces=(), held_as=jnp.bfloat16):
    values = jax.random.normal(stream_key, shape, jnp.float32) * spread
    if len(pieces) > 0:
        values = shard_levels(stream_key, shape, pieces, -0.22, 0.18) * values
    return jnp.clip(values, min=-most, max=most).astype(held_as)


def setup_inputs(seed: int = 0) -> dict:
    splits = jax.random.split(jax.random.key(seed), 7)
    spectra = centred(splits[0], (TRUNC, 2, FL, TRUNC), (1.0 / (2 * TRUNC) ** 0.5), 0.15625, ((0, 64), (2, 4)))
    legendre = centred(splits[1], (TRUNC, TRUNC, TRUNC), TRUNC ** -0.5, 0.25, ((0, 64),))
    block_mask = draw_block_mask(jax.random.fold_in(splits[6], 71), 0)
    wave_slot = draw_wave_slot(jax.random.fold_in(splits[6], 71), 0)
    lat_order = jax.random.permutation(splits[4], NLAT).astype(jnp.int32)
    level_order = jax.random.permutation(splits[5], FL).astype(jnp.int32)
    return dict(spectra=spectra, legendre=legendre, block_mask=block_mask, wave_slot=wave_slot, lat_order=lat_order, level_order=level_order)


def expand_mask(mask_slot):
    grown = jnp.repeat(jnp.repeat(mask_slot, BLOCK, axis=0), BLOCK, axis=1)
    return grown[:TRUNC, :TRUNC] > 0


def one_slot(packed):
    spec_slot, legendre_slot, mask_slot, wavenum = packed
    degree = jnp.arange(TRUNC, dtype=jnp.int32)
    kept_poly = jnp.where(expand_mask(mask_slot), legendre_slot.astype(jnp.float32), jnp.float32(0.0))
    upper_spec = jnp.where(degree >= wavenum, spec_slot.astype(jnp.float32), jnp.float32(0.0))
    parity_sign = jnp.where((degree + wavenum) % 2 == 0, jnp.float32(1.0), jnp.float32(-1.0))
    flat_rows = upper_spec.reshape(2 * FL, TRUNC)
    northern = jnp.dot(flat_rows, kept_poly, precision=lax.Precision.HIGHEST, preferred_element_type=jnp.float32)
    southern = jnp.dot(flat_rows * parity_sign, kept_poly, precision=lax.Precision.HIGHEST, preferred_element_type=jnp.float32)
    merged = jnp.concatenate([northern, southern[:, ::-1]], axis=1).astype(jnp.bfloat16)
    return merged.reshape(2, FL, 2 * TRUNC)


def reference(spectra, legendre, block_mask, wave_slot, lat_order, level_order):
    coeffs = lax.map(one_slot, (spectra, legendre, block_mask, wave_slot))
    coeffs = coeffs[:, :, :, lat_order]
    ordered = jnp.zeros_like(coeffs).at[wave_slot].set(coeffs).astype(jnp.float32)
    spectrum = lax.complex(ordered[:, 0], ordered[:, 1])
    spectrum = jnp.transpose(spectrum, (2, 1, 0))
    values = jnp.fft.irfft(spectrum, n=NLON, axis=-1) * NLON
    return values[:, level_order, :].astype(jnp.bfloat16)
```

```python
import math

import jax
import jax.numpy as jnp
import numpy as np
from jax import lax
from jax.experimental import pallas as pl
from jax.experimental.pallas import tpu as pltpu
from jax.sharding import PartitionSpec as P

MESH = pl.DeviceIdType.MESH
BF = jnp.bfloat16
F32 = jnp.float32

NLON = 3072
TRUNC = 640
NLAT = 1280
BLOCK = 64
NB = 10
WAVES = 64
FIELDS = 4
SLOTS = 10
LEV = 40
ROWS = 20
HALF = NLON // 2
QUART = NLON // 4

CH = 4
KG = 5
SC = 2 * SLOTS
SCP = 24
TW = 6
NT = 11
KP = NT * 128
BR = 2 * ROWS


def basis_table():
    q = np.arange(QUART)
    parts = []
    for odd in (0, 1):
        m = np.arange(odd, TRUNC, 2)
        ang = 2.0 * math.pi * ((m[:, None] * q[None, :]) % NLON) / NLON
        wt = np.where(m == 0, 1.0, 2.0)[:, None]
        parts += [wt * np.cos(ang), -wt * np.sin(ang)]
    return np.concatenate(parts, axis=0).astype(np.float32).astype(BF)


def regroup_matrix():
    mat = np.zeros((TW * 128, KG * 128), np.float32)
    for j in range(TW):
        for k in range(KG):
            for s in range(SC):
                mat[128 * j + SCP * k + s, 128 * k + SC * j + s] = 1.0
    return mat.astype(BF)


def level_columns():
    f, c, k, g, i = np.meshgrid(np.arange(FIELDS), np.arange(CH), np.arange(KG), np.arange(2), np.arange(4), indexing="ij")
    return (LEV * f + 2 * KG * c + KG * g + k + 1000 * i).reshape(1, -1).astype(np.float32)


def column_of(row_vec):
    return jnp.transpose(jnp.broadcast_to(row_vec, (128, row_vec.shape[1])))


def onehot_rows(ref, row_vec, cols):
    col = column_of(row_vec)
    lane = lax.broadcasted_iota(jnp.int32, col.shape, 1).astype(F32)
    for j in range(cols // 128):
        ref[:, j * 128 : (j + 1) * 128] = (col == lane + float(128 * j)).astype(F32).astype(BF)


def legendre_kernel(ws_ref, spec_ref, leg_ref, mask_ref, vlat_ref, out_ref, kept, z, oht):
    s = pl.program_id(0)
    wavenum = ws_ref[SLOTS * lax.axis_index("wave") + s]

    @pl.when(s == 0)
    def _():
        onehot_rows(oht, vlat_ref[...], NLAT)
        for g in range(2 * CH):
            for k in range(KG):
                at = 128 * g + SCP * k + 16
                z[:, at : at + 8, :] = jnp.zeros((NLAT // 128, 8, 128), F32)
            at = 128 * g + SCP * KG
            z[:, at : at + 8, :] = jnp.zeros((NLAT // 128, 8, 128), F32)

    jb = lax.broadcasted_iota(jnp.int32, (NB, TRUNC), 0) * BLOCK
    jj = lax.broadcasted_iota(jnp.int32, (NB, TRUNC), 1)
    widen = ((jj >= jb) & (jj < jb + BLOCK)).astype(F32)
    lanes = jnp.dot((mask_ref[0] > 0).astype(F32), widen, preferred_element_type=F32).astype(BF)
    for b in range(NB):
        kept[b * BLOCK : (b + 1) * BLOCK, :] = leg_ref[0, b * BLOCK : (b + 1) * BLOCK, :] * lanes[b : b + 1, :]
    degree = lax.broadcasted_iota(jnp.int32, (1, TRUNC), 1)
    upper = degree >= wavenum
    even = ((degree + wavenum) & 1) == 0
    spec = spec_ref[0].reshape(2 * LEV, TRUNC)
    spec_e = spec * jnp.where(upper & even, 1.0, 0.0).astype(BF)
    spec_o = spec * jnp.where(upper & ~even, 1.0, 0.0).astype(BF)
    both = jnp.dot(jnp.concatenate([spec_e, spec_o], axis=0), kept[...], preferred_element_type=F32)
    sums_e, sums_o = both[: 2 * LEV], both[2 * LEV :]
    north, south = sums_e + sums_o, sums_e - sums_o
    for comp in range(2):
        for g in range(2 * CH):
            src = slice(LEV * comp + KG * g, LEV * comp + KG * g + KG)
            dst = pl.ds(128 * g + 2 * s + comp, KG, stride=SCP)
            for t in range(TRUNC // 128):
                z[t, dst, :] = north[src, t * 128 : (t + 1) * 128]
                z[t + TRUNC // 128, dst, :] = south[src, t * 128 : (t + 1) * 128]

    @pl.when(s == SLOTS - 1)
    def _():
        low = lax.broadcasted_iota(jnp.int32, (NLAT // 8, 8, 128), 1) < 4
        for c in range(CH):
            zc = jnp.concatenate([z[t, 256 * c : 256 * (c + 1), :] for t in range(NLAT // 128)], axis=1).astype(BF)
            rows = lax.dot_general(oht[...], zc, (((1,), (1,)), ((), ())), preferred_element_type=F32)
            first = rows[:, :128].reshape(NLAT // 8, 8, 128)
            second = rows[:, 128:].reshape(NLAT // 8, 8, 128)
            tile_a = jnp.where(low, first, pltpu.roll(second, 4, 1))
            tile_b = jnp.where(low, pltpu.roll(first, 4, 1), second)
            tiles = jnp.stack([tile_a, tile_b], axis=1).reshape(WAVES, BR, 128)
            out_ref[c] = tiles.astype(BF)


def legendre_call(wave_slot, spectra, legendre, block_mask, vlat):
    return pl.pallas_call(
        legendre_kernel,
        out_shape=jax.ShapeDtypeStruct((CH, WAVES, BR, 128), BF),
        grid_spec=pltpu.PrefetchScalarGridSpec(
            num_scalar_prefetch=1,
            grid=(SLOTS,),
            in_specs=[
                pl.BlockSpec((1, 2, LEV, TRUNC), lambda s, ws: (s, 0, 0, 0)),
                pl.BlockSpec((1, TRUNC, TRUNC), lambda s, ws: (s, 0, 0)),
                pl.BlockSpec((1, NB, NB), lambda s, ws: (s, 0, 0)),
                pl.BlockSpec((1, NLAT), lambda s, ws: (0, 0)),
            ],
            out_specs=pl.BlockSpec((CH, WAVES, BR, 128), lambda s, ws: (0, 0, 0, 0)),
            scratch_shapes=[
                pltpu.VMEM((TRUNC, TRUNC), BF),
                pltpu.VMEM((NLAT // 128, 2 * CH * 128, 128), F32),
                pltpu.VMEM((NLAT, NLAT), BF),
            ],
        ),
        compiler_params=pltpu.CompilerParams(dimension_semantics=("arbitrary",), vmem_limit_bytes=56 << 20),
        name="legendre",
    )(wave_slot, spectra, legendre, block_mask, vlat)


def build_tables(basis, t_even, t_odd):
    n = TRUNC // 2
    t_even[:, :QUART] = basis[:TRUNC, :]
    t_odd[:, :QUART] = basis[TRUNC:, :]
    row = lax.broadcasted_iota(jnp.int32, (n, 1), 0)
    sign = jnp.where((row & 1) == 0, 1.0, -1.0).astype(F32)
    t_even[:n, QUART:] = (basis[:n, :].astype(F32) * sign).astype(BF)
    t_even[n:, QUART:] = (basis[n : 2 * n, :].astype(F32) * sign).astype(BF)
    t_odd[:n, QUART:] = (basis[3 * n :, :].astype(F32) * sign).astype(BF)
    t_odd[n:, QUART:] = (basis[2 * n : 3 * n, :].astype(F32) * -sign).astype(BF)


def fourier_chunk(recv_c, regroup, lhs, perm, t_even, t_odd, put):
    blocks = jnp.concatenate([recv_c[:, j].reshape(NT * BR, 128) for j in range(TW)], axis=1)
    moved = jnp.dot(blocks, regroup[...], preferred_element_type=F32)
    for k in range(KG):
        for t in range(NT):
            lhs[k * BR : (k + 1) * BR, t * 128 : (t + 1) * 128] = moved[
                t * BR : (t + 1) * BR, k * 128 : (k + 1) * 128
            ].astype(BF)
    ordered = jnp.dot(lhs[...], perm[...], preferred_element_type=F32).astype(BF)
    for h in range(2):
        cols = slice(h * QUART, (h + 1) * QUART)
        g_even = jnp.dot(ordered[:, :TRUNC], t_even[:, cols], preferred_element_type=F32)
        g_odd = jnp.dot(ordered[:, TRUNC:], t_odd[:, cols], preferred_element_type=F32)
        put(h, (g_even + g_odd).astype(BF).reshape(KG, BR, QUART))
        put(h + 2, (g_even - g_odd).astype(BF).reshape(KG, BR, QUART))


def exchange_kernel(
    send_ref, order_ref, basis_ref, regroup_ref, out_ref,
    recv, basis, regroup, perm, t_even, t_odd, lhs, quarters,
    load_sem, send_sem, recv_sem, xsend_sem, xrecv_sem,
):
    w, f = lax.axis_index("wave"), lax.axis_index("field")
    load_b = pltpu.make_async_copy(basis_ref, basis, load_sem.at[0])
    load_b.start()
    load_r = pltpu.make_async_copy(regroup_ref, regroup, load_sem.at[1])
    load_r.start()

    barrier = pltpu.get_barrier_semaphore()

    @pl.loop(1, WAVES)
    def _(d):
        pl.semaphore_signal(barrier, inc=1, device_id=(lax.rem(w + d, WAVES), f), device_id_type=MESH)

    for d in range(1, FIELDS):
        pl.semaphore_signal(barrier, inc=1, device_id=(w, lax.rem(f + d, FIELDS)), device_id_type=MESH)
    pl.semaphore_wait(barrier, WAVES + FIELDS - 2)

    my_tile, my_place = w // TW, lax.rem(w, TW)

    def wave_copy(c, peer):
        return pltpu.make_async_remote_copy(
            src_ref=send_ref.at[c, peer],
            dst_ref=recv.at[c, my_tile, my_place],
            send_sem=send_sem,
            recv_sem=recv_sem.at[c],
            device_id=(peer, f),
            device_id_type=MESH,
        )

    for c in range(CH):
        pltpu.make_async_copy(send_ref.at[c, w], recv.at[c, my_tile, my_place], recv_sem.at[c]).start()

        @pl.loop(1, WAVES // 2)
        def _(d):
            wave_copy(c, lax.rem(w + d, WAVES)).start()
            wave_copy(c, lax.rem(w + WAVES - d, WAVES)).start()

        wave_copy(c, lax.rem(w + WAVES // 2, WAVES)).start()

    for c in range(CH):
        for j in range(WAVES - TW * (NT - 1), TW):
            recv[c, NT - 1, j] = jnp.zeros((BR, 128), BF)
    onehot_rows(perm, order_ref[...], NLAT)
    load_b.wait()
    load_r.wait()
    build_tables(basis, t_even, t_odd)

    for c in range(CH):
        full = send_ref.at[c]
        pltpu.make_async_copy(full, full, recv_sem.at[c]).wait()

        def put(q, value):
            quarters[c, q] = value

        fourier_chunk(recv.at[c], regroup, lhs, perm, t_even, t_odd, put)
        pltpu.make_async_copy(quarters.at[c, f], out_ref.at[f, c], xrecv_sem).start()
        for d in range(1, FIELDS):
            peer = lax.rem(f + d, FIELDS)
            pltpu.make_async_remote_copy(
                src_ref=quarters.at[c, peer],
                dst_ref=out_ref.at[f, c],
                send_sem=xsend_sem,
                recv_sem=xrecv_sem,
                device_id=(w, peer),
                device_id_type=MESH,
            ).start()

    pltpu.make_async_copy(out_ref, out_ref, xrecv_sem).wait()
    sent = quarters.at[:, pl.ds(0, FIELDS - 1)]
    pltpu.make_async_copy(sent, sent, xsend_sem).wait()
    out_blocks = send_ref.at[:, pl.ds(0, WAVES - 1)]
    pltpu.make_async_copy(out_blocks, out_blocks, send_sem).wait()


def exchange_call(send, order):
    anyspace = pl.BlockSpec(memory_space=pl.ANY)
    return pl.pallas_call(
        exchange_kernel,
        out_shape=jax.ShapeDtypeStruct((FIELDS, CH, KG, BR, QUART), BF),
        in_specs=[anyspace, pl.BlockSpec(memory_space=pltpu.VMEM), anyspace, anyspace],
        out_specs=anyspace,
        scratch_shapes=[
            pltpu.VMEM((CH, NT, TW, BR, 128), BF),
            pltpu.VMEM((2 * TRUNC, QUART), BF),
            pltpu.VMEM((TW * 128, KG * 128), BF),
            pltpu.VMEM((KP, NLAT), BF),
            pltpu.VMEM((TRUNC, HALF), BF),
            pltpu.VMEM((TRUNC, HALF), BF),
            pltpu.VMEM((KG * BR, KP), BF),
            pltpu.VMEM((CH, FIELDS, KG, BR, QUART), BF),
            pltpu.SemaphoreType.DMA((2,)),
            pltpu.SemaphoreType.DMA,
            pltpu.SemaphoreType.DMA((CH,)),
            pltpu.SemaphoreType.DMA,
            pltpu.SemaphoreType.DMA,
        ],
        compiler_params=pltpu.CompilerParams(collective_id=0, has_side_effects=True, vmem_limit_bytes=56 << 20),
        name="exchange",
    )(send, order, jnp.asarray(basis_table()), jnp.asarray(regroup_matrix()))


def level_kernel(grid_ref, rowkey_ref, colkey_ref, out_ref, pick):
    @pl.when(pl.program_id(0) == 0)
    def _():
        col = column_of(rowkey_ref[...])
        for j in range(LEV * FIELDS * 4 // 128):
            pick[:, j * 128 : (j + 1) * 128] = (
                (col == colkey_ref[:, j * 128 : (j + 1) * 128]).astype(F32).astype(BF)
            )

    rows = grid_ref[...].reshape(FIELDS * CH * KG * 8, QUART)
    out = jnp.dot(pick[...], rows, preferred_element_type=F32)
    out_ref[...] = out.astype(BF).reshape(4, FIELDS * LEV, QUART)


def level_call(grid, rowkey):
    n = FIELDS * LEV * 4
    return pl.pallas_call(
        level_kernel,
        out_shape=jax.ShapeDtypeStruct((ROWS, FIELDS * LEV, QUART), BF),
        grid=(ROWS // 4,),
        in_specs=[
            pl.BlockSpec((FIELDS, CH, KG, 8, QUART), lambda i: (0, 0, 0, i, 0)),
            pl.BlockSpec((1, n), lambda i: (0, 0)),
            pl.BlockSpec((1, n), lambda i: (0, 0)),
        ],
        out_specs=pl.BlockSpec((4, FIELDS * LEV, QUART), lambda i: (i, 0, 0)),
        scratch_shapes=[pltpu.VMEM((n, n), BF)],
        compiler_params=pltpu.CompilerParams(dimension_semantics=("arbitrary",), vmem_limit_bytes=40 << 20),
        name="levels",
    )(grid, rowkey, jnp.asarray(level_columns()))


def index_rows(wave_slot, lat_order, level_order):
    vlat = jnp.where(lat_order < TRUNC, lat_order, NLAT + TRUNC - 1 - lat_order).astype(F32).reshape(1, NLAT)
    comp = jnp.arange(2, dtype=jnp.int32)
    place = TRUNC * (wave_slot & 1)[:, None] + (TRUNC // 2) * comp[None, :] + (wave_slot >> 1)[:, None]
    place = place.reshape(WAVES, SC).astype(F32)
    place = jnp.pad(place, ((0, NT * TW - WAVES), (0, 0)), constant_values=-1.0).reshape(NT, TW * SC)
    order = jnp.pad(place, ((0, 0), (0, 128 - TW * SC)), constant_values=-1.0).reshape(1, KP)
    rowkey = (level_order[None, :] + 1000 * jnp.arange(4, dtype=jnp.int32)[:, None]).astype(F32).reshape(1, -1)
    return vlat, order, rowkey


def shards(spectra, legendre, block_mask, wave_slot, lat_order, level_order):
    vlat, order, rowkey = index_rows(wave_slot, lat_order, level_order)
    send = legendre_call(wave_slot, spectra, legendre, block_mask, vlat)
    grid = exchange_call(send, order)
    return level_call(grid, rowkey)


def solution(mesh):
    placed = (
        P("wave", None, "field", None),
        P("wave", None, None),
        P("wave", None, None),
        P(),
        P(),
        P(),
    )
    return jax.shard_map(
        shards, mesh=mesh, in_specs=placed, out_specs=P("wave", None, "field"), check_vma=False
    )
```

```python
import math

import jax
import jax.numpy as jnp
import numpy as np
from jax import lax
from jax.experimental import pallas as pl
from jax.experimental.pallas import tpu as pltpu
from jax.sharding import PartitionSpec as P

MESH = pl.DeviceIdType.MESH
BF = jnp.bfloat16
F32 = jnp.float32

NLON = 3072
TRUNC = 640
NLAT = 1280
BLOCK = 64
NB = 10
WAVES = 64
FIELDS = 4
SLOTS = 10
LEV = 40
ROWS = 20
HALF = NLON // 2
QUART = NLON // 4

CH = 5
RW = ROWS // CH
KG = 6
NG = 7
SC = 2 * SLOTS
TW = 6
NT = 11
KP = NT * 128
MR = RW * LEV
CUT = 3
LT = NLAT // 128
PIECES = [(0, 0, CUT), (0, CUT, NG)] + [(c, 0, NG) for c in range(1, CH)]


def row_runs():
    runs, at = [], 0
    for low, high in ((0, CUT), (CUT, NG)):
        for k in range(KG):
            top = min(high, (LEV - k + KG - 1) // KG)
            runs.append((k, low, top, at))
            at += RW * (top - low)
    return runs


def basis_table():
    q = np.arange(QUART)
    parts = []
    for odd in (0, 1):
        m = np.arange(odd, TRUNC, 2)
        ang = 2.0 * math.pi * ((m[:, None] * q[None, :]) % NLON) / NLON
        wt = np.where(m == 0, 1.0, 2.0)[:, None]
        parts += [wt * np.cos(ang), -wt * np.sin(ang)]
    return np.concatenate(parts, axis=0).astype(np.float32).astype(BF)


def key_rows():
    keys = np.full((2, TW * 128), -1.0, np.float32)
    for j in range(TW):
        for k in range(KG):
            for s in range(SC):
                keys[0, 128 * j + SC * k + s] = 128 * k + 60 * (s // SLOTS) + SLOTS * j + s % SLOTS
    for f in range(FIELDS):
        for k, low, top, at in row_runs():
            for g in range(low, top):
                for i in range(RW):
                    keys[1, MR * f + at + RW * (g - low) + i] = LEV * f + KG * g + k + 1000 * i
    return keys


def column_of(row_vec):
    return jnp.transpose(jnp.broadcast_to(row_vec, (128, row_vec.shape[1])))


def columns_of(rows):
    return jnp.concatenate([column_of(rows[t : t + 1, :]) for t in range(rows.shape[0])], axis=0)


def fill_onehot(ref, col, cols):
    lane = lax.broadcasted_iota(jnp.int32, col.shape, 1).astype(F32)
    for j in range(cols // 128):
        ref[:, j * 128 : (j + 1) * 128] = (col == lane + float(128 * j)).astype(F32).astype(BF)


def clear_pads(z):
    for g in range(NG):
        z[:, 128 * g + SC * KG : 128 * (g + 1), :] = jnp.zeros((LT, 128 - SC * KG, 128), F32)
    first = 128 * (NG - 1) + SC * (LEV - KG * (NG - 1))
    z[:, first : 128 * NG, :] = jnp.zeros((LT, 128 * NG - first, 128), F32)


def legendre_slot(s, wavenum, spec, leg, mask, kept, z):
    jb = lax.broadcasted_iota(jnp.int32, (NB, TRUNC), 0) * BLOCK
    jj = lax.broadcasted_iota(jnp.int32, (NB, TRUNC), 1)
    widen = ((jj >= jb) & (jj < jb + BLOCK)).astype(F32)
    lanes = jnp.dot((mask[s] > 0).astype(F32), widen, preferred_element_type=F32).astype(BF)
    for b in range(NB):
        kept[b * BLOCK : (b + 1) * BLOCK, :] = leg[s, b * BLOCK : (b + 1) * BLOCK, :] * lanes[b : b + 1, :]
    degree = lax.broadcasted_iota(jnp.int32, (1, TRUNC), 1)
    upper = degree >= wavenum
    even = ((degree + wavenum) & 1) == 0
    rows = spec[s].reshape(2 * LEV, TRUNC)
    rows_e = rows * jnp.where(upper & even, 1.0, 0.0).astype(BF)
    rows_o = rows * jnp.where(upper & ~even, 1.0, 0.0).astype(BF)
    both = jnp.dot(jnp.concatenate([rows_e, rows_o], axis=0), kept[...], preferred_element_type=F32)
    sums_e, sums_o = both[: 2 * LEV], both[2 * LEV :]
    north, south = sums_e + sums_o, sums_e - sums_o
    for comp in range(2):
        for g in range(NG):
            n = min(KG, LEV - KG * g)
            src = slice(LEV * comp + KG * g, LEV * comp + KG * g + n)
            dst = pl.ds(128 * g + SLOTS * comp + s, n, stride=SC)
            for t in range(TRUNC // 128):
                z[t, dst, :] = north[src, t * 128 : (t + 1) * 128]
                z[t + TRUNC // 128, dst, :] = south[src, t * 128 : (t + 1) * 128]


def pack_chunk(c, vcol, oht, zb, send):
    fill_onehot(oht, vcol[pl.ds(c, NLAT // CH, stride=CH), :], NLAT)
    rows = lax.dot_general(oht[...], zb[...], (((1,), (1,)), ((), ())), preferred_element_type=F32)
    for g in range(NG):
        send[c, :, g] = rows[:, 128 * g : 128 * (g + 1)].reshape(WAVES, RW, 128).astype(BF)


def fill_order(slots, keycol, perm):
    m = columns_of(slots[...])
    half = jnp.floor(m * 0.5)
    key = TRUNC * (m - 2.0 * half) + half
    keycol[...] = jnp.full((KP, 128), -1.0, F32)
    for t in range(NT):
        n = min(TW * SLOTS, TRUNC - TW * SLOTS * t)
        part = key[TW * SLOTS * t : TW * SLOTS * t + n]
        for comp in range(2):
            keycol[128 * t + 60 * comp : 128 * t + 60 * comp + n, :] = part + float(TRUNC // 2 * comp)
    fill_onehot(perm, keycol[...], NLAT)


def fill_tables(basis, t_even, t_odd):
    n = TRUNC // 2
    t_even[:, :QUART] = basis[:TRUNC, :]
    t_odd[:, :QUART] = basis[TRUNC:, :]
    row = lax.broadcasted_iota(jnp.int32, (n, 1), 0)
    sign = jnp.where((row & 1) == 0, 1.0, -1.0).astype(F32)
    t_even[:n, QUART:] = (basis[:n, :].astype(F32) * sign).astype(BF)
    t_even[n:, QUART:] = (basis[n : 2 * n, :].astype(F32) * sign).astype(BF)
    t_odd[:n, QUART:] = (basis[3 * n :, :].astype(F32) * sign).astype(BF)
    t_odd[n:, QUART:] = (basis[2 * n : 3 * n, :].astype(F32) * -sign).astype(BF)


def fourier_piece(c, low, high, recv, regroup, lhs, perm, t_even, t_odd, quarters):
    ng = high - low
    blocks = jnp.concatenate(
        [recv[c, :, j, low:high].reshape(NT * ng * RW, 128) for j in range(TW)], axis=1
    )
    moved = jnp.dot(blocks, regroup[...], preferred_element_type=F32)
    runs = [r for r in row_runs() if low <= r[1] and r[1] < high]
    first = runs[0][3]
    last = first
    for k, start, top, at in runs:
        n = RW * (top - start)
        last = at + n
        for t in range(NT):
            src = t * ng * RW + RW * (start - low)
            lhs[at : at + n, t * 128 : (t + 1) * 128] = moved[src : src + n, k * 128 : (k + 1) * 128]
    ordered = jnp.dot(lhs[first:last, :].astype(BF), perm[...], preferred_element_type=F32).astype(BF)
    for h in range(2):
        cols = slice(h * QUART, (h + 1) * QUART)
        g_even = jnp.dot(ordered[:, :TRUNC], t_even[:, cols], preferred_element_type=F32)
        g_odd = jnp.dot(ordered[:, TRUNC:], t_odd[:, cols], preferred_element_type=F32)
        quarters[c, h, first:last, :] = (g_even + g_odd).astype(BF)
        quarters[c, h + 2, first:last, :] = (g_even - g_odd).astype(BF)
    return first, last - first


def fill_levels(levels, colkey, pick):
    col = columns_of(levels[...])[: FIELDS * LEV]
    for i in range(RW):
        for j in range(FIELDS * MR // 128):
            hit = col + float(1000 * i) == colkey[1:2, j * 128 : (j + 1) * 128]
            pick[FIELDS * LEV * i : FIELDS * LEV * (i + 1), j * 128 : (j + 1) * 128] = hit.astype(F32).astype(BF)


def transform_kernel(
    ws_ref, spec_ref, leg_ref, mask_ref, slots_ref, lats_ref, levels_ref, keys_ref, basis_ref, out_ref,
    spec, leg, kept, z, zb, vcol, oht, send, recv, basis, regroup, keycol, perm, t_even, t_odd, lhs,
    quarters, xrecv, pick, stage,
    leg_sem, load_sem, send_sem, recv_sem, xsend_sem, xrecv_sem, out_sem,
):
    w, f = lax.axis_index("wave"), lax.axis_index("field")
    loads = [pltpu.make_async_copy(spec_ref, spec, load_sem.at[0]), pltpu.make_async_copy(basis_ref, basis, load_sem.at[1])]
    slot_loads = [pltpu.make_async_copy(leg_ref.at[s], leg.at[s], leg_sem.at[s]) for s in range(SLOTS)]
    loads[0].start()
    for load in slot_loads:
        load.start()
    loads[1].start()

    barrier = pltpu.get_barrier_semaphore()

    @pl.loop(1, WAVES)
    def _(d):
        pl.semaphore_signal(barrier, inc=1, device_id=(lax.rem(w + d, WAVES), f), device_id_type=MESH)

    for d in range(1, FIELDS):
        pl.semaphore_signal(barrier, inc=1, device_id=(w, lax.rem(f + d, FIELDS)), device_id_type=MESH)

    lat = columns_of(lats_ref[...])
    vcol[...] = jnp.where(lat < TRUNC, lat, (NLAT + TRUNC - 1) - lat)
    clear_pads(z)
    loads[0].wait()

    @pl.loop(0, SLOTS)
    def _(s):
        pltpu.make_async_copy(leg_ref.at[s], leg.at[s], leg_sem.at[s]).wait()
        legendre_slot(s, ws_ref[SLOTS * w + s], spec, leg, mask_ref, kept, z)

    zb[...] = jnp.concatenate([z[t] for t in range(LT)], axis=1).astype(BF)

    my_tile, my_place = w // TW, lax.rem(w, TW)

    def wave_copy(p, peer):
        c, low, high = PIECES[p]
        return pltpu.make_async_remote_copy(
            src_ref=send.at[c, peer, pl.ds(low, high - low)],
            dst_ref=recv.at[c, my_tile, my_place, pl.ds(low, high - low)],
            send_sem=send_sem,
            recv_sem=recv_sem.at[p],
            device_id=(peer, f),
            device_id_type=MESH,
        )

    for p, (c, low, high) in enumerate(PIECES):
        if low == 0:
            pack_chunk(c, vcol, oht, zb, send)
        if p == 0:
            pl.semaphore_wait(barrier, WAVES + FIELDS - 2)
        span = pl.ds(low, high - low)
        pltpu.make_async_copy(send.at[c, w, span], recv.at[c, my_tile, my_place, span], recv_sem.at[p]).start()

        @pl.loop(1, WAVES // 2)
        def _(d):
            wave_copy(p, lax.rem(w + d, WAVES)).start()
            wave_copy(p, lax.rem(w + WAVES - d, WAVES)).start()

        wave_copy(p, lax.rem(w + WAVES // 2, WAVES)).start()

    for c in range(CH):
        for j in range(WAVES - TW * (NT - 1), TW):
            recv[c, NT - 1, j] = jnp.zeros((NG, RW, 128), BF)
    fill_onehot(regroup, column_of(keys_ref[0:1, :]), KG * 128)
    fill_order(slots_ref, keycol, perm)
    loads[1].wait()
    fill_tables(basis, t_even, t_odd)
    fill_levels(levels_ref, keys_ref, pick)

    def out_copies(c):
        return [pltpu.make_async_copy(stage.at[c % 2, i], out_ref.at[CH * i + c], out_sem.at[c % 2, i]) for i in range(RW)]

    def finish_chunk(c):
        pltpu.make_async_copy(xrecv.at[c], xrecv.at[c], xrecv_sem.at[c]).wait()
        rows = xrecv[c].reshape(FIELDS * MR, QUART)
        if c >= 2:
            for copy in out_copies(c - 2):
                copy.wait()
        values = jnp.dot(pick[...], rows, preferred_element_type=F32).astype(BF)
        stage[c % 2] = values.reshape(RW, FIELDS * LEV, QUART)
        for copy in out_copies(c):
            copy.start()

    for p, (c, low, high) in enumerate(PIECES):
        landed = send.at[c, :, pl.ds(low, high - low)]
        pltpu.make_async_copy(landed, landed, recv_sem.at[p]).wait()
        first, count = fourier_piece(c, low, high, recv, regroup, lhs, perm, t_even, t_odd, quarters)
        part = pl.ds(first, count)
        pltpu.make_async_copy(quarters.at[c, f, part], xrecv.at[c, f, part], xrecv_sem.at[c]).start()
        for d in range(1, FIELDS):
            peer = lax.rem(f + d, FIELDS)
            pltpu.make_async_remote_copy(
                src_ref=quarters.at[c, peer, part],
                dst_ref=xrecv.at[c, f, part],
                send_sem=xsend_sem,
                recv_sem=xrecv_sem.at[c],
                device_id=(w, peer),
                device_id_type=MESH,
            ).start()
        if high == NG and c >= 1:
            finish_chunk(c - 1)
    finish_chunk(CH - 1)

    for c in (CH - 2, CH - 1):
        for copy in out_copies(c):
            copy.wait()
    sent = quarters.at[:, pl.ds(0, FIELDS - 1)]
    pltpu.make_async_copy(sent, sent, xsend_sem).wait()
    left = send.at[:, pl.ds(0, WAVES - 1)]
    pltpu.make_async_copy(left, left, send_sem).wait()


def shards(spectra, legendre, block_mask, wave_slot, lat_order, level_order):
    slots = wave_slot.astype(F32).reshape(TRUNC // 128, 128)
    lats = lat_order.astype(F32).reshape(LT, 128)
    levels = jnp.pad(level_order, (0, 256 - FIELDS * LEV)).astype(F32).reshape(2, 128)
    anyspace = pl.BlockSpec(memory_space=pl.ANY)
    vmem = pl.BlockSpec(memory_space=pltpu.VMEM)
    return pl.pallas_call(
        transform_kernel,
        out_shape=jax.ShapeDtypeStruct((ROWS, FIELDS * LEV, QUART), BF),
        in_specs=[pl.BlockSpec(memory_space=pltpu.SMEM), anyspace, anyspace, vmem, vmem, vmem, vmem, vmem, anyspace],
        out_specs=anyspace,
        scratch_shapes=[
            pltpu.VMEM((SLOTS, 2, LEV, TRUNC), BF),
            pltpu.VMEM((SLOTS, TRUNC, TRUNC), BF),
            pltpu.VMEM((TRUNC, TRUNC), BF),
            pltpu.VMEM((LT, NG * 128, 128), F32),
            pltpu.VMEM((NG * 128, NLAT), BF),
            pltpu.VMEM((NLAT, 128), F32),
            pltpu.VMEM((NLAT // CH, NLAT), BF),
            pltpu.VMEM((CH, WAVES, NG, RW, 128), BF),
            pltpu.VMEM((CH, NT, TW, NG, RW, 128), BF),
            pltpu.VMEM((2 * TRUNC, QUART), BF),
            pltpu.VMEM((TW * 128, KG * 128), BF),
            pltpu.VMEM((KP, 128), F32),
            pltpu.VMEM((KP, NLAT), BF),
            pltpu.VMEM((TRUNC, HALF), BF),
            pltpu.VMEM((TRUNC, HALF), BF),
            pltpu.VMEM((MR, KP), F32),
            pltpu.VMEM((CH, FIELDS, MR, QUART), BF),
            pltpu.VMEM((CH, FIELDS, MR, QUART), BF),
            pltpu.VMEM((RW * FIELDS * LEV, FIELDS * MR), BF),
            pltpu.VMEM((2, RW, FIELDS * LEV, QUART), BF),
            pltpu.SemaphoreType.DMA((SLOTS,)),
            pltpu.SemaphoreType.DMA((2,)),
            pltpu.SemaphoreType.DMA,
            pltpu.SemaphoreType.DMA((len(PIECES),)),
            pltpu.SemaphoreType.DMA,
            pltpu.SemaphoreType.DMA((CH,)),
            pltpu.SemaphoreType.DMA((2, RW)),
        ],
        compiler_params=pltpu.CompilerParams(collective_id=0, has_side_effects=True, vmem_limit_bytes=60 << 20),
        name="transform",
    )(wave_slot, spectra, legendre, block_mask, slots, lats, levels, jnp.asarray(key_rows()), jnp.asarray(basis_table()))


def solution(mesh):
    placed = (
        P("wave", None, "field", None),
        P("wave", None, None),
        P("wave", None, None),
        P(),
        P(),
        P(),
    )
    return jax.shard_map(
        shards, mesh=mesh, in_specs=placed, out_specs=P("wave", None, "field"), check_vma=False
    )
```

```python
import math

import jax
import jax.numpy as jnp
import numpy as np
from jax import lax
from jax.experimental import pallas as pl
from jax.experimental.pallas import tpu as pltpu
from jax.sharding import PartitionSpec as P

MESH = pl.DeviceIdType.MESH
BF = jnp.bfloat16
F32 = jnp.float32

NLON = 3072
TRUNC = 640
NLAT = 1280
BLOCK = 64
NB = 10
WAVES = 64
FIELDS = 4
SLOTS = 10
LEV = 40
ROWS = 20
HALF = NLON // 2
QUART = NLON // 4

CH = 5
RW = ROWS // CH
KG = 6
NG = 7
SC = 2 * SLOTS
TW = 6
NT = 11
KP = NT * 128
MR = RW * LEV
CUT = 3
LT = NLAT // 128
PIECES = [(0, CUT), (CUT, NG)]


def row_runs():
    runs, at = [], 0
    for low, high in PIECES:
        for k in range(KG):
            top = min(high, (LEV - k + KG - 1) // KG)
            runs.append((k, low, top, at))
            at += RW * (top - low)
    return runs


def basis_table():
    q = np.arange(QUART)
    parts = []
    for odd in (0, 1):
        m = np.arange(odd, TRUNC, 2)
        ang = 2.0 * math.pi * ((m[:, None] * q[None, :]) % NLON) / NLON
        wt = np.where(m == 0, 1.0, 2.0)[:, None]
        parts += [wt * np.cos(ang), -wt * np.sin(ang)]
    return np.concatenate(parts, axis=0).astype(np.float32).astype(BF)


def key_rows():
    keys = np.full((2, TW * 128), -1.0, np.float32)
    for j in range(TW):
        for k in range(KG):
            for s in range(SC):
                keys[0, 128 * j + SC * k + s] = 128 * k + 60 * (s // SLOTS) + SLOTS * j + s % SLOTS
    for f in range(FIELDS):
        for k, low, top, at in row_runs():
            for g in range(low, top):
                for i in range(RW):
                    keys[1, MR * f + at + RW * (g - low) + i] = LEV * f + KG * g + k + 1000 * i
    return keys


def column_of(row_vec):
    return jnp.transpose(jnp.broadcast_to(row_vec, (128, row_vec.shape[1])))


def columns_of(rows):
    rows = rows.astype(F32)
    return jnp.concatenate([column_of(rows[t : t + 1, :]) for t in range(rows.shape[0])], axis=0)


def fill_onehot(ref, col, cols):
    lane = lax.broadcasted_iota(jnp.int32, col.shape, 1).astype(F32)
    for j in range(cols // 128):
        ref[:, j * 128 : (j + 1) * 128] = (col == lane + float(128 * j)).astype(F32).astype(BF)


def clear_pads(z):
    for g in range(NG):
        z[:, 128 * g + SC * KG : 128 * (g + 1), :] = jnp.zeros((LT, 128 - SC * KG, 128), F32)
    first = 128 * (NG - 1) + SC * (LEV - KG * (NG - 1))
    z[:, first : 128 * NG, :] = jnp.zeros((LT, 128 * NG - first, 128), F32)


def legendre_slot(s, wavenum, spec, leg, mask, kept, z):
    jb = lax.broadcasted_iota(jnp.int32, (NB, TRUNC), 0) * BLOCK
    jj = lax.broadcasted_iota(jnp.int32, (NB, TRUNC), 1)
    widen = ((jj >= jb) & (jj < jb + BLOCK)).astype(F32)
    lanes = jnp.dot((mask[s] > 0).astype(F32), widen, preferred_element_type=F32).astype(BF)
    for b in range(NB):
        kept[b * BLOCK : (b + 1) * BLOCK, :] = leg[s, b * BLOCK : (b + 1) * BLOCK, :] * lanes[b : b + 1, :]
    degree = lax.broadcasted_iota(jnp.int32, (1, TRUNC), 1)
    upper = degree >= wavenum
    even = ((degree + wavenum) & 1) == 0
    rows = spec[s].reshape(2 * LEV, TRUNC)
    rows_e = rows * jnp.where(upper & even, 1.0, 0.0).astype(BF)
    rows_o = rows * jnp.where(upper & ~even, 1.0, 0.0).astype(BF)
    both = jnp.dot(jnp.concatenate([rows_e, rows_o], axis=0), kept[...], preferred_element_type=F32)
    sums_e, sums_o = both[: 2 * LEV], both[2 * LEV :]
    north, south = sums_e + sums_o, sums_e - sums_o
    for comp in range(2):
        for g in range(NG):
            n = min(KG, LEV - KG * g)
            src = slice(LEV * comp + KG * g, LEV * comp + KG * g + n)
            dst = pl.ds(128 * g + SLOTS * comp + s, n, stride=SC)
            for t in range(TRUNC // 128):
                z[t, dst, :] = north[src, t * 128 : (t + 1) * 128]
                z[t + TRUNC // 128, dst, :] = south[src, t * 128 : (t + 1) * 128]


def pack_chunk(c, vcol, oht, zb, send):
    fill_onehot(oht, vcol[pl.ds(c, NLAT // CH, stride=CH), :], NLAT)
    rows = lax.dot_general(oht[...], zb[...], (((1,), (1,)), ((), ())), preferred_element_type=F32)
    for g in range(NG):
        send[c, :, g] = rows[:, 128 * g : 128 * (g + 1)].reshape(WAVES, RW, 128).astype(BF)


def fill_order(slots, keycol, perm):
    m = columns_of(slots[...])
    half = jnp.floor(m * 0.5)
    key = TRUNC * (m - 2.0 * half) + half
    keycol[...] = jnp.full((KP, 128), -1.0, F32)
    for t in range(NT):
        n = min(TW * SLOTS, TRUNC - TW * SLOTS * t)
        part = key[TW * SLOTS * t : TW * SLOTS * t + n]
        for comp in range(2):
            keycol[128 * t + 60 * comp : 128 * t + 60 * comp + n, :] = part + float(TRUNC // 2 * comp)
    fill_onehot(perm, keycol[...], NLAT)


def fill_tables(basis, t_even, t_odd):
    n = TRUNC // 2
    t_even[:, :QUART] = basis[:TRUNC, :]
    t_odd[:, :QUART] = basis[TRUNC:, :]
    row = lax.broadcasted_iota(jnp.int32, (n, 1), 0)
    sign = jnp.where((row & 1) == 0, 1.0, -1.0).astype(F32)
    t_even[:n, QUART:] = (basis[:n, :].astype(F32) * sign).astype(BF)
    t_even[n:, QUART:] = (basis[n : 2 * n, :].astype(F32) * sign).astype(BF)
    t_odd[:n, QUART:] = (basis[3 * n :, :].astype(F32) * sign).astype(BF)
    t_odd[n:, QUART:] = (basis[2 * n : 3 * n, :].astype(F32) * -sign).astype(BF)


def fourier_piece(c, low, high, recv, regroup, lhs, perm, t_even, t_odd, quarters):
    ng = high - low
    blocks = jnp.concatenate(
        [recv[c, :, j, low:high].reshape(NT * ng * RW, 128) for j in range(TW)], axis=1
    )
    moved = jnp.dot(blocks, regroup[...], preferred_element_type=F32)
    runs = [r for r in row_runs() if low <= r[1] and r[1] < high]
    first = runs[0][3]
    last = first
    for k, start, top, at in runs:
        n = RW * (top - start)
        last = at + n
        for t in range(NT):
            src = t * ng * RW + RW * (start - low)
            lhs[at : at + n, t * 128 : (t + 1) * 128] = moved[src : src + n, k * 128 : (k + 1) * 128]
    ordered = jnp.dot(lhs[first:last, :].astype(BF), perm[...], preferred_element_type=F32).astype(BF)
    for h in range(2):
        cols = slice(h * QUART, (h + 1) * QUART)
        g_even = jnp.dot(ordered[:, :TRUNC], t_even[:, cols], preferred_element_type=F32)
        g_odd = jnp.dot(ordered[:, TRUNC:], t_odd[:, cols], preferred_element_type=F32)
        quarters[c, h, first:last, :] = (g_even + g_odd).astype(BF)
        quarters[c, h + 2, first:last, :] = (g_even - g_odd).astype(BF)
    return first, last - first


def fill_levels(levels, column, colkey, pick):
    @pl.loop(0, FIELDS * LEV)
    def _(k):
        column[pl.ds(k, 1), :] = jnp.full((1, 128), levels[k].astype(F32), F32)

    col = column[: FIELDS * LEV, :]
    for i in range(RW):
        for j in range(FIELDS * MR // 128):
            hit = col + float(1000 * i) == colkey[1:2, j * 128 : (j + 1) * 128]
            pick[FIELDS * LEV * i : FIELDS * LEV * (i + 1), j * 128 : (j + 1) * 128] = hit.astype(F32).astype(BF)


def transform_kernel(
    ws_ref, spec_ref, leg_ref, mask_ref, slots_ref, lats_ref, levels_ref, keys_ref, basis_ref, out_ref,
    spec, leg, kept, z, zb, vcol, oht, send, recv, basis, regroup, keycol, perm, t_even, t_odd, lhs,
    quarters, xrecv, pick, stage,
    leg_sem, load_sem, send_sem, recv_sem, xsend_sem, xrecv_sem, out_sem,
):
    w, f = lax.axis_index("wave"), lax.axis_index("field")
    loads = [pltpu.make_async_copy(spec_ref, spec, load_sem.at[0]), pltpu.make_async_copy(basis_ref, basis, load_sem.at[1])]
    slot_loads = [pltpu.make_async_copy(leg_ref.at[s], leg.at[s], leg_sem.at[s]) for s in range(SLOTS)]
    loads[0].start()
    for load in slot_loads:
        load.start()
    loads[1].start()

    barrier = pltpu.get_barrier_semaphore()

    @pl.loop(1, WAVES)
    def _(d):
        pl.semaphore_signal(barrier, inc=1, device_id=(lax.rem(w + d, WAVES), f), device_id_type=MESH)

    for d in range(1, FIELDS):
        pl.semaphore_signal(barrier, inc=1, device_id=(w, lax.rem(f + d, FIELDS)), device_id_type=MESH)

    lat = columns_of(lats_ref[...])
    vcol[...] = jnp.where(lat < TRUNC, lat, (NLAT + TRUNC - 1) - lat)
    clear_pads(z)
    loads[0].wait()

    @pl.loop(0, SLOTS)
    def _(s):
        pltpu.make_async_copy(leg_ref.at[s], leg.at[s], leg_sem.at[s]).wait()
        legendre_slot(s, ws_ref[SLOTS * w + s], spec, leg, mask_ref, kept, z)

    zb[...] = jnp.concatenate([z[t] for t in range(LT)], axis=1).astype(BF)
    pl.semaphore_wait(barrier, WAVES + FIELDS - 2)
    my_tile, my_place = w // TW, lax.rem(w, TW)

    def wave_copy(c, p, peer):
        span = pl.ds(PIECES[p][0], PIECES[p][1] - PIECES[p][0])
        return pltpu.make_async_remote_copy(
            src_ref=send.at[c, peer, span],
            dst_ref=recv.at[c, my_tile, my_place, span],
            send_sem=send_sem,
            recv_sem=recv_sem.at[c, p],
            device_id=(peer, f),
            device_id_type=MESH,
        )

    @pl.loop(0, CH)
    def _(c):
        pack_chunk(c, vcol, oht, zb, send)
        for p, (low, high) in enumerate(PIECES):
            span = pl.ds(low, high - low)
            pltpu.make_async_copy(send.at[c, w, span], recv.at[c, my_tile, my_place, span], recv_sem.at[c, p]).start()

            @pl.loop(1, WAVES // 2)
            def _(d):
                wave_copy(c, p, lax.rem(w + d, WAVES)).start()
                wave_copy(c, p, lax.rem(w + WAVES - d, WAVES)).start()

            wave_copy(c, p, lax.rem(w + WAVES // 2, WAVES)).start()

    for c in range(CH):
        for j in range(WAVES - TW * (NT - 1), TW):
            recv[c, NT - 1, j] = jnp.zeros((NG, RW, 128), BF)
    fill_onehot(regroup, column_of(keys_ref[0:1, :]), KG * 128)
    fill_order(slots_ref, keycol, perm)
    loads[1].wait()
    fill_tables(basis, t_even, t_odd)
    fill_levels(levels_ref, keycol, keys_ref, pick)

    def out_copies(c):
        slot = lax.rem(c, 2)
        return [pltpu.make_async_copy(stage.at[slot, i], out_ref.at[CH * i + c], out_sem.at[slot, i]) for i in range(RW)]

    def finish_chunk(c):
        pltpu.make_async_copy(xrecv.at[c], xrecv.at[c], xrecv_sem.at[c]).wait()
        rows = xrecv[c].reshape(FIELDS * MR, QUART)

        @pl.when(c >= 2)
        def _():
            for copy in out_copies(c - 2):
                copy.wait()

        values = jnp.dot(pick[...], rows, preferred_element_type=F32).astype(BF)
        stage[lax.rem(c, 2)] = values.reshape(RW, FIELDS * LEV, QUART)
        for copy in out_copies(c):
            copy.start()

    @pl.loop(0, CH)
    def _(c):
        for p, (low, high) in enumerate(PIECES):
            landed = send.at[c, :, pl.ds(low, high - low)]
            pltpu.make_async_copy(landed, landed, recv_sem.at[c, p]).wait()
            first, count = fourier_piece(c, low, high, recv, regroup, lhs, perm, t_even, t_odd, quarters)
            part = pl.ds(first, count)
            pltpu.make_async_copy(quarters.at[c, f, part], xrecv.at[c, f, part], xrecv_sem.at[c]).start()
            for d in (1, 3, 2):
                peer = lax.rem(f + d, FIELDS)
                pltpu.make_async_remote_copy(
                    src_ref=quarters.at[c, peer, part],
                    dst_ref=xrecv.at[c, f, part],
                    send_sem=xsend_sem,
                    recv_sem=xrecv_sem.at[c],
                    device_id=(w, peer),
                    device_id_type=MESH,
                ).start()

        @pl.when(c >= 1)
        def _():
            finish_chunk(c - 1)

    finish_chunk(jnp.int32(CH - 1))
    for c in (CH - 2, CH - 1):
        for copy in out_copies(jnp.int32(c)):
            copy.wait()
    sent = quarters.at[:, pl.ds(0, FIELDS - 1)]
    pltpu.make_async_copy(sent, sent, xsend_sem).wait()
    left = send.at[:, pl.ds(0, WAVES - 1)]
    pltpu.make_async_copy(left, left, send_sem).wait()


def shards(spectra, legendre, block_mask, wave_slot, lat_order, level_order):
    slots = wave_slot.reshape(TRUNC // 128, 128)
    lats = lat_order.reshape(LT, 128)
    anyspace = pl.BlockSpec(memory_space=pl.ANY)
    vmem = pl.BlockSpec(memory_space=pltpu.VMEM)
    smem = pl.BlockSpec(memory_space=pltpu.SMEM)
    return pl.pallas_call(
        transform_kernel,
        out_shape=jax.ShapeDtypeStruct((ROWS, FIELDS * LEV, QUART), BF),
        in_specs=[smem, anyspace, anyspace, vmem, vmem, vmem, smem, vmem, anyspace],
        out_specs=anyspace,
        scratch_shapes=[
            pltpu.VMEM((SLOTS, 2, LEV, TRUNC), BF),
            pltpu.VMEM((SLOTS, TRUNC, TRUNC), BF),
            pltpu.VMEM((TRUNC, TRUNC), BF),
            pltpu.VMEM((LT, NG * 128, 128), F32),
            pltpu.VMEM((NG * 128, NLAT), BF),
            pltpu.VMEM((NLAT, 128), F32),
            pltpu.VMEM((NLAT // CH, NLAT), BF),
            pltpu.VMEM((CH, WAVES, NG, RW, 128), BF),
            pltpu.VMEM((CH, NT, TW, NG, RW, 128), BF),
            pltpu.VMEM((2 * TRUNC, QUART), BF),
            pltpu.VMEM((TW * 128, KG * 128), BF),
            pltpu.VMEM((KP, 128), F32),
            pltpu.VMEM((KP, NLAT), BF),
            pltpu.VMEM((TRUNC, HALF), BF),
            pltpu.VMEM((TRUNC, HALF), BF),
            pltpu.VMEM((MR, KP), F32),
            pltpu.VMEM((CH, FIELDS, MR, QUART), BF),
            pltpu.VMEM((CH, FIELDS, MR, QUART), BF),
            pltpu.VMEM((RW * FIELDS * LEV, FIELDS * MR), BF),
            pltpu.VMEM((2, RW, FIELDS * LEV, QUART), BF),
            pltpu.SemaphoreType.DMA((SLOTS,)),
            pltpu.SemaphoreType.DMA((2,)),
            pltpu.SemaphoreType.DMA,
            pltpu.SemaphoreType.DMA((CH, len(PIECES))),
            pltpu.SemaphoreType.DMA,
            pltpu.SemaphoreType.DMA((CH,)),
            pltpu.SemaphoreType.DMA((2, RW)),
        ],
        compiler_params=pltpu.CompilerParams(collective_id=0, has_side_effects=True, vmem_limit_bytes=60 << 20),
        name="transform",
    )(wave_slot, spectra, legendre, block_mask, slots, lats, level_order, jnp.asarray(key_rows()), jnp.asarray(basis_table()))


def solution(mesh):
    placed = (
        P("wave", None, "field", None),
        P("wave", None, None),
        P("wave", None, None),
        P(),
        P(),
        P(),
    )
    return jax.shard_map(
        shards, mesh=mesh, in_specs=placed, out_specs=P("wave", None, "field"), check_vma=False
    )
```

```python
import math

import jax
import jax.numpy as jnp
import numpy as np
from jax import lax
from jax.experimental import pallas as pl
from jax.experimental.pallas import tpu as pltpu
from jax.sharding import PartitionSpec as P

MESH = pl.DeviceIdType.MESH
BF = jnp.bfloat16
F32 = jnp.float32

NLON = 3072
TRUNC = 640
NLAT = 1280
BLOCK = 64
NB = 10
WAVES = 64
FIELDS = 4
SLOTS = 10
LEV = 40
ROWS = 20
HALF = NLON // 2
QUART = NLON // 4

CH = 5
RW = ROWS // CH
KG = 6
NG = 7
SC = 2 * SLOTS
TW = 6
NT = 11
KP = NT * 128
MR = RW * LEV
CUT = 3
LT = NLAT // 128
GREET = 7
PIECES = [(0, CUT), (CUT, NG)]


def row_runs():
    runs, at = [], 0
    for low, high in PIECES:
        for k in range(KG):
            top = min(high, (LEV - k + KG - 1) // KG)
            runs.append((k, low, top, at))
            at += RW * (top - low)
    return runs


def basis_table():
    q = np.arange(QUART)
    parts = []
    for odd in (0, 1):
        m = np.arange(odd, TRUNC, 2)
        ang = 2.0 * math.pi * ((m[:, None] * q[None, :]) % NLON) / NLON
        wt = np.where(m == 0, 1.0, 2.0)[:, None]
        parts += [wt * np.cos(ang), -wt * np.sin(ang)]
    return np.concatenate(parts, axis=0).astype(np.float32).astype(BF)


def key_rows():
    keys = np.full((2, TW * 128), -1.0, np.float32)
    for j in range(TW):
        for k in range(KG):
            for s in range(SC):
                keys[0, 128 * j + SC * k + s] = 128 * k + 60 * (s // SLOTS) + SLOTS * j + s % SLOTS
    for f in range(FIELDS):
        for k, low, top, at in row_runs():
            for g in range(low, top):
                for i in range(RW):
                    keys[1, MR * f + at + RW * (g - low) + i] = LEV * f + KG * g + k + 1000 * i
    return keys


def column_of(row_vec):
    return jnp.transpose(jnp.broadcast_to(row_vec, (128, row_vec.shape[1])))


def columns_of(rows):
    rows = rows.astype(F32)
    return jnp.concatenate([column_of(rows[t : t + 1, :]) for t in range(rows.shape[0])], axis=0)


def fill_onehot(ref, col, cols):
    lane = lax.broadcasted_iota(jnp.int32, col.shape, 1).astype(F32)
    for j in range(cols // 128):
        ref[:, j * 128 : (j + 1) * 128] = (col == lane + float(128 * j)).astype(F32).astype(BF)


def clear_pads(z):
    for g in range(NG):
        z[:, 128 * g + SC * KG : 128 * (g + 1), :] = jnp.zeros((LT, 128 - SC * KG, 128), F32)
    first = 128 * (NG - 1) + SC * (LEV - KG * (NG - 1))
    z[:, first : 128 * NG, :] = jnp.zeros((LT, 128 * NG - first, 128), F32)


def legendre_slot(s, wavenum, spec, leg, mask, kept, z):
    jb = lax.broadcasted_iota(jnp.int32, (NB, TRUNC), 0) * BLOCK
    jj = lax.broadcasted_iota(jnp.int32, (NB, TRUNC), 1)
    widen = ((jj >= jb) & (jj < jb + BLOCK)).astype(F32)
    lanes = jnp.dot((mask[s] > 0).astype(F32), widen, preferred_element_type=F32).astype(BF)
    for b in range(NB):
        kept[b * BLOCK : (b + 1) * BLOCK, :] = leg[s, b * BLOCK : (b + 1) * BLOCK, :] * lanes[b : b + 1, :]
    degree = lax.broadcasted_iota(jnp.int32, (1, TRUNC), 1)
    upper = degree >= wavenum
    even = ((degree + wavenum) & 1) == 0
    rows = spec[s].reshape(2 * LEV, TRUNC)
    rows_e = rows * jnp.where(upper & even, 1.0, 0.0).astype(BF)
    rows_o = rows * jnp.where(upper & ~even, 1.0, 0.0).astype(BF)
    both = jnp.dot(jnp.concatenate([rows_e, rows_o], axis=0), kept[...], preferred_element_type=F32)
    sums_e, sums_o = both[: 2 * LEV], both[2 * LEV :]
    north, south = sums_e + sums_o, sums_e - sums_o
    for comp in range(2):
        for g in range(NG):
            n = min(KG, LEV - KG * g)
            src = slice(LEV * comp + KG * g, LEV * comp + KG * g + n)
            dst = pl.ds(128 * g + SLOTS * comp + s, n, stride=SC)
            for t in range(TRUNC // 128):
                z[t, dst, :] = north[src, t * 128 : (t + 1) * 128]
                z[t + TRUNC // 128, dst, :] = south[src, t * 128 : (t + 1) * 128]


def pack_chunk(c, vcol, oht, zb, send):
    fill_onehot(oht, vcol[pl.ds(c, NLAT // CH, stride=CH), :], NLAT)
    rows = lax.dot_general(oht[...], zb[...], (((1,), (1,)), ((), ())), preferred_element_type=F32)
    for g in range(NG):
        send[c, :, g] = rows[:, 128 * g : 128 * (g + 1)].reshape(WAVES, RW, 128).astype(BF)


def fill_order(slots, keycol, perm):
    m = columns_of(slots[...])
    half = jnp.floor(m * 0.5)
    key = TRUNC * (m - 2.0 * half) + half
    keycol[...] = jnp.full((KP, 128), -1.0, F32)
    for t in range(NT):
        n = min(TW * SLOTS, TRUNC - TW * SLOTS * t)
        part = key[TW * SLOTS * t : TW * SLOTS * t + n]
        for comp in range(2):
            keycol[128 * t + 60 * comp : 128 * t + 60 * comp + n, :] = part + float(TRUNC // 2 * comp)
    fill_onehot(perm, keycol[...], NLAT)


def fill_tables(basis, t_even, t_odd):
    n = TRUNC // 2
    t_even[:, :QUART] = basis[:TRUNC, :]
    t_odd[:, :QUART] = basis[TRUNC:, :]
    row = lax.broadcasted_iota(jnp.int32, (n, 1), 0)
    sign = jnp.where((row & 1) == 0, 1.0, -1.0).astype(F32)
    t_even[:n, QUART:] = (basis[:n, :].astype(F32) * sign).astype(BF)
    t_even[n:, QUART:] = (basis[n : 2 * n, :].astype(F32) * sign).astype(BF)
    t_odd[:n, QUART:] = (basis[3 * n :, :].astype(F32) * sign).astype(BF)
    t_odd[n:, QUART:] = (basis[2 * n : 3 * n, :].astype(F32) * -sign).astype(BF)


def fourier_piece(c, low, high, recv, regroup, lhs, perm, t_even, t_odd, quarters):
    ng = high - low
    blocks = jnp.concatenate(
        [recv[c, :, j, low:high].reshape(NT * ng * RW, 128) for j in range(TW)], axis=1
    )
    moved = jnp.dot(blocks, regroup[...], preferred_element_type=F32)
    runs = [r for r in row_runs() if low <= r[1] and r[1] < high]
    first = runs[0][3]
    last = first
    for k, start, top, at in runs:
        n = RW * (top - start)
        last = at + n
        for t in range(NT):
            src = t * ng * RW + RW * (start - low)
            lhs[at : at + n, t * 128 : (t + 1) * 128] = moved[src : src + n, k * 128 : (k + 1) * 128]
    ordered = jnp.dot(lhs[first:last, :].astype(BF), perm[...], preferred_element_type=F32).astype(BF)
    for h in range(2):
        cols = slice(h * QUART, (h + 1) * QUART)
        g_even = jnp.dot(ordered[:, :TRUNC], t_even[:, cols], preferred_element_type=F32)
        g_odd = jnp.dot(ordered[:, TRUNC:], t_odd[:, cols], preferred_element_type=F32)
        quarters[c, h, first:last, :] = (g_even + g_odd).astype(BF)
        quarters[c, h + 2, first:last, :] = (g_even - g_odd).astype(BF)
    return first, last - first


def fill_levels(levels, column, colkey, pick):
    @pl.loop(0, FIELDS * LEV)
    def _(k):
        column[pl.ds(k, 1), :] = jnp.full((1, 128), levels[k].astype(F32), F32)

    col = column[: FIELDS * LEV, :]
    for i in range(RW):
        for j in range(FIELDS * MR // 128):
            hit = col + float(1000 * i) == colkey[1:2, j * 128 : (j + 1) * 128]
            pick[FIELDS * LEV * i : FIELDS * LEV * (i + 1), j * 128 : (j + 1) * 128] = hit.astype(F32).astype(BF)


def transform_kernel(
    ws_ref, spec_ref, leg_ref, mask_ref, slots_ref, lats_ref, levels_ref, keys_ref, basis_ref, out_ref,
    spec, leg, kept, z, zb, vcol, oht, send, recv, basis, regroup, keycol, perm, t_even, t_odd, lhs,
    quarters, xrecv, pick,
    leg_sem, load_sem, send_sem, recv_sem, xsend_sem, xrecv_sem,
):
    w, f = lax.axis_index("wave"), lax.axis_index("field")
    loads = [pltpu.make_async_copy(spec_ref, spec, load_sem.at[0]), pltpu.make_async_copy(basis_ref, basis, load_sem.at[1])]
    slot_loads = [pltpu.make_async_copy(leg_ref.at[s], leg.at[s], leg_sem.at[s]) for s in range(SLOTS)]
    loads[0].start()
    for load in slot_loads:
        load.start()
    loads[1].start()

    barrier = pltpu.get_barrier_semaphore()
    for d in range(1, FIELDS):
        pl.semaphore_signal(barrier, inc=1, device_id=(w, lax.rem(f + d, FIELDS)), device_id_type=MESH)

    lat = columns_of(lats_ref[...])
    vcol[...] = jnp.where(lat < TRUNC, lat, (NLAT + TRUNC - 1) - lat)
    clear_pads(z)
    loads[0].wait()

    @pl.loop(0, SLOTS)
    def _(s):
        @pl.when(s < (WAVES - 1) // GREET)
        def _():
            for t in range(GREET):
                peer = lax.rem(w + GREET * s + t + 1, WAVES)
                pl.semaphore_signal(barrier, inc=1, device_id=(peer, f), device_id_type=MESH)

        pltpu.make_async_copy(leg_ref.at[s], leg.at[s], leg_sem.at[s]).wait()
        legendre_slot(s, ws_ref[SLOTS * w + s], spec, leg, mask_ref, kept, z)

    zb[...] = jnp.concatenate([z[t] for t in range(LT)], axis=1).astype(BF)
    pl.semaphore_wait(barrier, WAVES + FIELDS - 2)
    my_tile, my_place = w // TW, lax.rem(w, TW)

    def wave_copy(c, p, peer):
        span = pl.ds(PIECES[p][0], PIECES[p][1] - PIECES[p][0])
        return pltpu.make_async_remote_copy(
            src_ref=send.at[c, peer, span],
            dst_ref=recv.at[c, my_tile, my_place, span],
            send_sem=send_sem,
            recv_sem=recv_sem.at[c, p],
            device_id=(peer, f),
            device_id_type=MESH,
        )

    def send_chunk(c):
        pack_chunk(c, vcol, oht, zb, send)
        for p, (low, high) in enumerate(PIECES):
            span = pl.ds(low, high - low)
            pltpu.make_async_copy(send.at[c, w, span], recv.at[c, my_tile, my_place, span], recv_sem.at[c, p]).start()

            @pl.loop(1, WAVES // 2)
            def _(d):
                wave_copy(c, p, lax.rem(w + d, WAVES)).start()
                wave_copy(c, p, lax.rem(w + WAVES - d, WAVES)).start()

            wave_copy(c, p, lax.rem(w + WAVES // 2, WAVES)).start()

    send_chunk(0)
    for c in range(CH):
        for j in range(WAVES - TW * (NT - 1), TW):
            recv[c, NT - 1, j] = jnp.zeros((NG, RW, 128), BF)
    fill_onehot(regroup, column_of(keys_ref[0:1, :]), KG * 128)
    fill_order(slots_ref, keycol, perm)
    loads[1].wait()
    fill_tables(basis, t_even, t_odd)
    send_chunk(1)
    fill_levels(levels_ref, keycol, keys_ref, pick)

    def finish_chunk(c):
        pltpu.make_async_copy(xrecv.at[c], xrecv.at[c], xrecv_sem.at[c]).wait()
        rows = xrecv[c].reshape(FIELDS * MR, QUART)
        values = jnp.dot(pick[...], rows, preferred_element_type=F32).astype(BF)
        for i in range(RW):
            out_ref[CH * i + c] = values[FIELDS * LEV * i : FIELDS * LEV * (i + 1), :]

    @pl.loop(0, CH)
    def _(c):
        for p, (low, high) in enumerate(PIECES):
            landed = send.at[c, :, pl.ds(low, high - low)]
            pltpu.make_async_copy(landed, landed, recv_sem.at[c, p]).wait()
            first, count = fourier_piece(c, low, high, recv, regroup, lhs, perm, t_even, t_odd, quarters)
            part = pl.ds(first, count)
            pltpu.make_async_copy(quarters.at[c, f, part], xrecv.at[c, f, part], xrecv_sem.at[c]).start()
            for d in (1, 3, 2):
                peer = lax.rem(f + d, FIELDS)
                pltpu.make_async_remote_copy(
                    src_ref=quarters.at[c, peer, part],
                    dst_ref=xrecv.at[c, f, part],
                    send_sem=xsend_sem,
                    recv_sem=xrecv_sem.at[c],
                    device_id=(w, peer),
                    device_id_type=MESH,
                ).start()

        @pl.when(c + 2 < CH)
        def _():
            send_chunk(c + 2)

        @pl.when(c >= 1)
        def _():
            finish_chunk(c - 1)

    finish_chunk(CH - 1)
    sent = quarters.at[:, pl.ds(0, FIELDS - 1)]
    pltpu.make_async_copy(sent, sent, xsend_sem).wait()
    left = send.at[:, pl.ds(0, WAVES - 1)]
    pltpu.make_async_copy(left, left, send_sem).wait()


def shards(spectra, legendre, block_mask, wave_slot, lat_order, level_order):
    slots = wave_slot.reshape(TRUNC // 128, 128)
    lats = lat_order.reshape(LT, 128)
    anyspace = pl.BlockSpec(memory_space=pl.ANY)
    vmem = pl.BlockSpec(memory_space=pltpu.VMEM)
    smem = pl.BlockSpec(memory_space=pltpu.SMEM)
    return pl.pallas_call(
        transform_kernel,
        out_shape=pltpu.VMEM((ROWS, FIELDS * LEV, QUART), BF),
        in_specs=[smem, anyspace, anyspace, vmem, vmem, vmem, smem, vmem, anyspace],
        out_specs=vmem,
        scratch_shapes=[
            pltpu.VMEM((SLOTS, 2, LEV, TRUNC), BF),
            pltpu.VMEM((SLOTS, TRUNC, TRUNC), BF),
            pltpu.VMEM((TRUNC, TRUNC), BF),
            pltpu.VMEM((LT, NG * 128, 128), F32),
            pltpu.VMEM((NG * 128, NLAT), BF),
            pltpu.VMEM((NLAT, 128), F32),
            pltpu.VMEM((NLAT // CH, NLAT), BF),
            pltpu.VMEM((CH, WAVES, NG, RW, 128), BF),
            pltpu.VMEM((CH, NT, TW, NG, RW, 128), BF),
            pltpu.VMEM((2 * TRUNC, QUART), BF),
            pltpu.VMEM((TW * 128, KG * 128), BF),
            pltpu.VMEM((KP, 128), F32),
            pltpu.VMEM((KP, NLAT), BF),
            pltpu.VMEM((TRUNC, HALF), BF),
            pltpu.VMEM((TRUNC, HALF), BF),
            pltpu.VMEM((MR, KP), F32),
            pltpu.VMEM((CH, FIELDS, MR, QUART), BF),
            pltpu.VMEM((CH, FIELDS, MR, QUART), BF),
            pltpu.VMEM((RW * FIELDS * LEV, FIELDS * MR), BF),
            pltpu.SemaphoreType.DMA((SLOTS,)),
            pltpu.SemaphoreType.DMA((2,)),
            pltpu.SemaphoreType.DMA,
            pltpu.SemaphoreType.DMA((CH, len(PIECES))),
            pltpu.SemaphoreType.DMA,
            pltpu.SemaphoreType.DMA((CH,)),
        ],
        compiler_params=pltpu.CompilerParams(collective_id=0, has_side_effects=True, vmem_limit_bytes=57 << 20),
        name="transform",
    )(wave_slot, spectra, legendre, block_mask, slots, lats, level_order, jnp.asarray(key_rows()), jnp.asarray(basis_table()))


def solution(mesh):
    placed = (
        P("wave", None, "field", None),
        P("wave", None, None),
        P("wave", None, None),
        P(),
        P(),
        P(),
    )
    return jax.shard_map(
        shards, mesh=mesh, in_specs=placed, out_specs=P("wave", None, "field"), check_vma=False
    )
```

```python
import math

import jax
import jax.numpy as jnp
import numpy as np
from jax import lax
from jax.experimental import pallas as pl
from jax.experimental.pallas import tpu as pltpu
from jax.sharding import PartitionSpec as P

MESH = pl.DeviceIdType.MESH
BF = jnp.bfloat16
F32 = jnp.float32

NLON = 3072
TRUNC = 640
NLAT = 1280
BLOCK = 64
NB = 10
WAVES = 64
FIELDS = 4
SLOTS = 10
LEV = 40
ROWS = 20
HALF = NLON // 2
QUART = NLON // 4

CH = 5
RW = ROWS // CH
KG = 6
NG = 7
SC = 2 * SLOTS
TW = 6
NT = 11
KP = NT * 128
MR = RW * LEV
CUT = 3
LT = NLAT // 128
GREET = 21
PIECES = [(0, CUT), (CUT, NG)]


def row_runs():
    runs, at = [], 0
    for low, high in PIECES:
        for k in range(KG):
            top = min(high, (LEV - k + KG - 1) // KG)
            runs.append((k, low, top, at))
            at += RW * (top - low)
    return runs


def basis_table():
    q = np.arange(QUART)
    parts = []
    for odd in (0, 1):
        m = np.arange(odd, TRUNC, 2)
        ang = 2.0 * math.pi * ((m[:, None] * q[None, :]) % NLON) / NLON
        wt = np.where(m == 0, 1.0, 2.0)[:, None]
        parts += [wt * np.cos(ang), -wt * np.sin(ang)]
    return np.concatenate(parts, axis=0).astype(np.float32).astype(BF)


def key_rows():
    keys = np.full((2, TW * 128), -1.0, np.float32)
    for j in range(TW):
        for k in range(KG):
            for s in range(SC):
                keys[0, 128 * j + SC * k + s] = 128 * k + 60 * (s // SLOTS) + SLOTS * j + s % SLOTS
    for f in range(FIELDS):
        for k, low, top, at in row_runs():
            for g in range(low, top):
                for i in range(RW):
                    keys[1, MR * f + at + RW * (g - low) + i] = LEV * f + KG * g + k + 1000 * i
    return keys


def column_of(row_vec):
    return jnp.transpose(jnp.broadcast_to(row_vec, (128, row_vec.shape[1])))


def columns_of(rows):
    rows = rows.astype(F32)
    return jnp.concatenate([column_of(rows[t : t + 1, :]) for t in range(rows.shape[0])], axis=0)


def fill_onehot(ref, col, cols):
    lane = lax.broadcasted_iota(jnp.int32, col.shape, 1).astype(F32)
    for j in range(cols // 128):
        ref[:, j * 128 : (j + 1) * 128] = (col == lane + float(128 * j)).astype(F32).astype(BF)


def clear_pads(z):
    for g in range(NG):
        z[:, 128 * g + SC * KG : 128 * (g + 1), :] = jnp.zeros((LT, 128 - SC * KG, 128), F32)
    first = 128 * (NG - 1) + SC * (LEV - KG * (NG - 1))
    z[:, first : 128 * NG, :] = jnp.zeros((LT, 128 * NG - first, 128), F32)


def legendre_slot(s, wavenum, spec, leg, mask, kept, z):
    jb = lax.broadcasted_iota(jnp.int32, (NB, TRUNC), 0) * BLOCK
    jj = lax.broadcasted_iota(jnp.int32, (NB, TRUNC), 1)
    widen = ((jj >= jb) & (jj < jb + BLOCK)).astype(F32)
    lanes = jnp.dot((mask[s] > 0).astype(F32), widen, preferred_element_type=F32).astype(BF)
    for b in range(NB):
        kept[b * BLOCK : (b + 1) * BLOCK, :] = leg[s, b * BLOCK : (b + 1) * BLOCK, :] * lanes[b : b + 1, :]
    degree = lax.broadcasted_iota(jnp.int32, (1, TRUNC), 1)
    upper = degree >= wavenum
    even = ((degree + wavenum) & 1) == 0
    rows = spec[s].reshape(2 * LEV, TRUNC)
    rows_e = rows * jnp.where(upper & even, 1.0, 0.0).astype(BF)
    rows_o = rows * jnp.where(upper & ~even, 1.0, 0.0).astype(BF)
    both = jnp.dot(jnp.concatenate([rows_e, rows_o], axis=0), kept[...], preferred_element_type=F32)
    sums_e, sums_o = both[: 2 * LEV], both[2 * LEV :]
    north, south = sums_e + sums_o, sums_e - sums_o
    for comp in range(2):
        for g in range(NG):
            n = min(KG, LEV - KG * g)
            src = slice(LEV * comp + KG * g, LEV * comp + KG * g + n)
            dst = pl.ds(128 * g + SLOTS * comp + s, n, stride=SC)
            for t in range(TRUNC // 128):
                z[t, dst, :] = north[src, t * 128 : (t + 1) * 128]
                z[t + TRUNC // 128, dst, :] = south[src, t * 128 : (t + 1) * 128]


def round_piece(low, high, z, zb):
    part = slice(128 * low, 128 * high)
    for t in range(LT):
        zb[part, 128 * t : 128 * (t + 1)] = z[t, part, :].astype(BF)


def pack_piece(c, low, high, oht, zb, send):
    rows = lax.dot_general(
        oht[...], zb[128 * low : 128 * high, :], (((1,), (1,)), ((), ())), preferred_element_type=F32
    )
    for g in range(low, high):
        send[c, :, g] = rows[:, 128 * (g - low) : 128 * (g - low + 1)].reshape(WAVES, RW, 128).astype(BF)


def fill_order(slots, keycol, perm):
    m = columns_of(slots[...])
    half = jnp.floor(m * 0.5)
    key = TRUNC * (m - 2.0 * half) + half
    keycol[...] = jnp.full((KP, 128), -1.0, F32)
    for t in range(NT):
        n = min(TW * SLOTS, TRUNC - TW * SLOTS * t)
        part = key[TW * SLOTS * t : TW * SLOTS * t + n]
        for comp in range(2):
            keycol[128 * t + 60 * comp : 128 * t + 60 * comp + n, :] = part + float(TRUNC // 2 * comp)
    fill_onehot(perm, keycol[...], NLAT)


def fill_tables(basis, t_even, t_odd):
    n = TRUNC // 2
    t_even[:, :QUART] = basis[:TRUNC, :]
    t_odd[:, :QUART] = basis[TRUNC:, :]
    row = lax.broadcasted_iota(jnp.int32, (n, 1), 0)
    sign = jnp.where((row & 1) == 0, 1.0, -1.0).astype(F32)
    t_even[:n, QUART:] = (basis[:n, :].astype(F32) * sign).astype(BF)
    t_even[n:, QUART:] = (basis[n : 2 * n, :].astype(F32) * sign).astype(BF)
    t_odd[:n, QUART:] = (basis[3 * n :, :].astype(F32) * sign).astype(BF)
    t_odd[n:, QUART:] = (basis[2 * n : 3 * n, :].astype(F32) * -sign).astype(BF)


def fourier_piece(c, low, high, recv, regroup, lhs, perm, t_even, t_odd, quarters):
    ng = high - low
    blocks = jnp.concatenate(
        [recv[c, :, j, low:high].reshape(NT * ng * RW, 128) for j in range(TW)], axis=1
    )
    moved = jnp.dot(blocks, regroup[...], preferred_element_type=F32)
    runs = [r for r in row_runs() if low <= r[1] and r[1] < high]
    first = runs[0][3]
    last = first
    for k, start, top, at in runs:
        n = RW * (top - start)
        last = at + n
        for t in range(NT):
            src = t * ng * RW + RW * (start - low)
            lhs[at : at + n, t * 128 : (t + 1) * 128] = moved[src : src + n, k * 128 : (k + 1) * 128]
    ordered = jnp.dot(lhs[first:last, :].astype(BF), perm[...], preferred_element_type=F32).astype(BF)
    for h in range(2):
        cols = slice(h * QUART, (h + 1) * QUART)
        g_even = jnp.dot(ordered[:, :TRUNC], t_even[:, cols], preferred_element_type=F32)
        g_odd = jnp.dot(ordered[:, TRUNC:], t_odd[:, cols], preferred_element_type=F32)
        quarters[c, h, first:last, :] = (g_even + g_odd).astype(BF)
        quarters[c, h + 2, first:last, :] = (g_even - g_odd).astype(BF)
    return first, last - first


def fill_levels(levels, column, colkey, pick):
    @pl.loop(0, FIELDS * LEV)
    def _(k):
        column[pl.ds(k, 1), :] = jnp.full((1, 128), levels[k].astype(F32), F32)

    col = column[: FIELDS * LEV, :]
    for i in range(RW):
        for j in range(FIELDS * MR // 128):
            hit = col + float(1000 * i) == colkey[1:2, j * 128 : (j + 1) * 128]
            pick[FIELDS * LEV * i : FIELDS * LEV * (i + 1), j * 128 : (j + 1) * 128] = hit.astype(F32).astype(BF)


def transform_kernel(
    ws_ref, spec_ref, leg_ref, mask_ref, slots_ref, lats_ref, levels_ref, keys_ref, basis_ref, out_ref,
    spec, leg, kept, z, zb, vcol, oht, send, recv, basis, regroup, keycol, perm, t_even, t_odd, lhs,
    quarters, xrecv, pick,
    leg_sem, load_sem, send_sem, recv_sem, xsend_sem, xrecv_sem,
):
    w, f = lax.axis_index("wave"), lax.axis_index("field")
    loads = [pltpu.make_async_copy(spec_ref, spec, load_sem.at[0]), pltpu.make_async_copy(basis_ref, basis, load_sem.at[1])]
    slot_loads = [pltpu.make_async_copy(leg_ref.at[s], leg.at[s], leg_sem.at[s]) for s in range(SLOTS)]
    loads[0].start()
    for load in slot_loads:
        load.start()
    loads[1].start()

    barrier = pltpu.get_barrier_semaphore()
    for d in range(1, FIELDS):
        pl.semaphore_signal(barrier, inc=1, device_id=(w, lax.rem(f + d, FIELDS)), device_id_type=MESH)

    lat = columns_of(lats_ref[...])
    vcol[...] = jnp.where(lat < TRUNC, lat, (NLAT + TRUNC - 1) - lat)
    clear_pads(z)

    def choose_rows(c):
        fill_onehot(oht, vcol[pl.ds(c, NLAT // CH, stride=CH), :], NLAT)

    choose_rows(0)
    loads[0].wait()

    @pl.loop(0, SLOTS // 2)
    def _(pair):
        @pl.when(pair < (WAVES - 1) // GREET)
        def _():
            for t in range(GREET):
                peer = lax.rem(w + GREET * pair + t + 1, WAVES)
                pl.semaphore_signal(barrier, inc=1, device_id=(peer, f), device_id_type=MESH)

        for half in range(2):
            s = 2 * pair + half
            pltpu.make_async_copy(leg_ref.at[s], leg.at[s], leg_sem.at[s]).wait()
        for half in range(2):
            s = 2 * pair + half
            legendre_slot(s, ws_ref[SLOTS * w + s], spec, leg, mask_ref, kept.at[half], z)

    my_tile, my_place = w // TW, lax.rem(w, TW)

    def wave_copy(c, p, peer):
        span = pl.ds(PIECES[p][0], PIECES[p][1] - PIECES[p][0])
        return pltpu.make_async_remote_copy(
            src_ref=send.at[c, peer, span],
            dst_ref=recv.at[c, my_tile, my_place, span],
            send_sem=send_sem,
            recv_sem=recv_sem.at[c, p],
            device_id=(peer, f),
            device_id_type=MESH,
        )

    def send_piece(c, p):
        low, high = PIECES[p]
        span = pl.ds(low, high - low)
        pack_piece(c, low, high, oht, zb, send)
        pltpu.make_async_copy(send.at[c, w, span], recv.at[c, my_tile, my_place, span], recv_sem.at[c, p]).start()

        @pl.loop(1, WAVES // 2)
        def _(d):
            wave_copy(c, p, lax.rem(w + d, WAVES)).start()
            wave_copy(c, p, lax.rem(w + WAVES - d, WAVES)).start()

        wave_copy(c, p, lax.rem(w + WAVES // 2, WAVES)).start()

    def send_chunk(c):
        choose_rows(c)
        for p in range(len(PIECES)):
            send_piece(c, p)

    round_piece(*PIECES[0], z, zb)
    pl.semaphore_wait(barrier, WAVES + FIELDS - 2)
    send_piece(0, 0)
    round_piece(*PIECES[1], z, zb)
    fill_onehot(regroup, column_of(keys_ref[0:1, :]), KG * 128)
    send_piece(0, 1)
    for c in range(CH):
        for j in range(WAVES - TW * (NT - 1), TW):
            recv[c, NT - 1, j] = jnp.zeros((NG, RW, 128), BF)
    fill_order(slots_ref, keycol, perm)
    loads[1].wait()
    fill_tables(basis, t_even, t_odd)
    send_chunk(1)
    fill_levels(levels_ref, keycol, keys_ref, pick)

    def finish_chunk(c):
        pltpu.make_async_copy(xrecv.at[c], xrecv.at[c], xrecv_sem.at[c]).wait()
        rows = xrecv[c].reshape(FIELDS * MR, QUART)
        values = jnp.dot(pick[...], rows, preferred_element_type=F32).astype(BF)
        for i in range(RW):
            out_ref[CH * i + c] = values[FIELDS * LEV * i : FIELDS * LEV * (i + 1), :]

    @pl.loop(0, CH)
    def _(c):
        for p, (low, high) in enumerate(PIECES):
            landed = send.at[c, :, pl.ds(low, high - low)]
            pltpu.make_async_copy(landed, landed, recv_sem.at[c, p]).wait()
            first, count = fourier_piece(c, low, high, recv, regroup, lhs, perm, t_even, t_odd, quarters)
            part = pl.ds(first, count)
            pltpu.make_async_copy(quarters.at[c, f, part], xrecv.at[c, f, part], xrecv_sem.at[c]).start()
            for d in (1, 3, 2):
                peer = lax.rem(f + d, FIELDS)
                pltpu.make_async_remote_copy(
                    src_ref=quarters.at[c, peer, part],
                    dst_ref=xrecv.at[c, f, part],
                    send_sem=xsend_sem,
                    recv_sem=xrecv_sem.at[c],
                    device_id=(w, peer),
                    device_id_type=MESH,
                ).start()

        @pl.when(c + 2 < CH)
        def _():
            send_chunk(c + 2)

        @pl.when(c >= 1)
        def _():
            finish_chunk(c - 1)

    finish_chunk(CH - 1)
    sent = quarters.at[:, pl.ds(0, FIELDS - 1)]
    pltpu.make_async_copy(sent, sent, xsend_sem).wait()
    left = send.at[:, pl.ds(0, WAVES - 1)]
    pltpu.make_async_copy(left, left, send_sem).wait()


def shards(spectra, legendre, block_mask, wave_slot, lat_order, level_order):
    slots = wave_slot.reshape(TRUNC // 128, 128)
    lats = lat_order.reshape(LT, 128)
    anyspace = pl.BlockSpec(memory_space=pl.ANY)
    vmem = pl.BlockSpec(memory_space=pltpu.VMEM)
    smem = pl.BlockSpec(memory_space=pltpu.SMEM)
    return pl.pallas_call(
        transform_kernel,
        out_shape=pltpu.VMEM((ROWS, FIELDS * LEV, QUART), BF),
        in_specs=[smem, anyspace, anyspace, vmem, vmem, vmem, smem, vmem, anyspace],
        out_specs=vmem,
        scratch_shapes=[
            pltpu.VMEM((SLOTS, 2, LEV, TRUNC), BF),
            pltpu.VMEM((SLOTS, TRUNC, TRUNC), BF),
            pltpu.VMEM((2, TRUNC, TRUNC), BF),
            pltpu.VMEM((LT, NG * 128, 128), F32),
            pltpu.VMEM((NG * 128, NLAT), BF),
            pltpu.VMEM((NLAT, 128), F32),
            pltpu.VMEM((NLAT // CH, NLAT), BF),
            pltpu.VMEM((CH, WAVES, NG, RW, 128), BF),
            pltpu.VMEM((CH, NT, TW, NG, RW, 128), BF),
            pltpu.VMEM((2 * TRUNC, QUART), BF),
            pltpu.VMEM((TW * 128, KG * 128), BF),
            pltpu.VMEM((KP, 128), F32),
            pltpu.VMEM((KP, NLAT), BF),
            pltpu.VMEM((TRUNC, HALF), BF),
            pltpu.VMEM((TRUNC, HALF), BF),
            pltpu.VMEM((MR, KP), F32),
            pltpu.VMEM((CH, FIELDS, MR, QUART), BF),
            pltpu.VMEM((CH, FIELDS, MR, QUART), BF),
            pltpu.VMEM((RW * FIELDS * LEV, FIELDS * MR), BF),
            pltpu.SemaphoreType.DMA((SLOTS,)),
            pltpu.SemaphoreType.DMA((2,)),
            pltpu.SemaphoreType.DMA,
            pltpu.SemaphoreType.DMA((CH, len(PIECES))),
            pltpu.SemaphoreType.DMA,
            pltpu.SemaphoreType.DMA((CH,)),
        ],
        compiler_params=pltpu.CompilerParams(collective_id=0, has_side_effects=True, vmem_limit_bytes=57 << 20),
        name="transform",
    )(wave_slot, spectra, legendre, block_mask, slots, lats, level_order, jnp.asarray(key_rows()), jnp.asarray(basis_table()))


def solution(mesh):
    placed = (
        P("wave", None, "field", None),
        P("wave", None, None),
        P("wave", None, None),
        P(),
        P(),
        P(),
    )
    return jax.shard_map(
        shards, mesh=mesh, in_specs=placed, out_specs=P("wave", None, "field"), check_vma=False
    )
```

```python
import math

import jax
import jax.numpy as jnp
import numpy as np
from jax import lax
from jax.experimental import pallas as pl
from jax.experimental.pallas import tpu as pltpu
from jax.sharding import PartitionSpec as P

MESH = pl.DeviceIdType.MESH
BF = jnp.bfloat16
F32 = jnp.float32

NLON = 3072
TRUNC = 640
NLAT = 1280
BLOCK = 64
NB = 10
WAVES = 64
FIELDS = 4
SLOTS = 10
LEV = 40
ROWS = 20
HALF = NLON // 2
QUART = NLON // 4

CH = 5
RW = ROWS // CH
KG = 6
NG = 7
SC = 2 * SLOTS
TW = 6
NT = 11
KP = NT * 128
MR = RW * LEV
CUT = 3
LT = NLAT // 128
GREET = 21
PIECES = [(0, CUT), (CUT, NG)]


def row_runs():
    runs, at = [], 0
    for low, high in PIECES:
        for k in range(KG):
            top = min(high, (LEV - k + KG - 1) // KG)
            runs.append((k, low, top, at))
            at += RW * (top - low)
    return runs


def basis_table():
    q = np.arange(QUART)
    parts = []
    for odd in (0, 1):
        m = np.arange(odd, TRUNC, 2)
        ang = 2.0 * math.pi * ((m[:, None] * q[None, :]) % NLON) / NLON
        wt = np.where(m == 0, 1.0, 2.0)[:, None]
        parts += [wt * np.cos(ang), -wt * np.sin(ang)]
    return np.concatenate(parts, axis=0).astype(np.float32).astype(BF)


def key_rows():
    keys = np.full((2, TW * 128), -1.0, np.float32)
    for j in range(TW):
        for k in range(KG):
            for s in range(SC):
                keys[0, 128 * j + SC * k + s] = 128 * k + 60 * (s // SLOTS) + SLOTS * j + s % SLOTS
    for f in range(FIELDS):
        for k, low, top, at in row_runs():
            for g in range(low, top):
                for i in range(RW):
                    keys[1, MR * f + at + RW * (g - low) + i] = LEV * f + KG * g + k + 1000 * i
    return keys


def column_of(row_vec):
    return jnp.transpose(jnp.broadcast_to(row_vec, (128, row_vec.shape[1])))


def columns_of(rows):
    rows = rows.astype(F32)
    return jnp.concatenate([column_of(rows[t : t + 1, :]) for t in range(rows.shape[0])], axis=0)


def fill_onehot(ref, col, cols):
    lane = lax.broadcasted_iota(jnp.int32, col.shape, 1).astype(F32)
    for j in range(cols // 128):
        ref[:, j * 128 : (j + 1) * 128] = (col == lane + float(128 * j)).astype(F32).astype(BF)


def clear_pads(z):
    for g in range(NG):
        z[:, 128 * g + SC * KG : 128 * (g + 1), :] = jnp.zeros((LT, 128 - SC * KG, 128), F32)
    first = 128 * (NG - 1) + SC * (LEV - KG * (NG - 1))
    z[:, first : 128 * NG, :] = jnp.zeros((LT, 128 * NG - first, 128), F32)


def mask_slot(s, leg, mask):
    jb = lax.broadcasted_iota(jnp.int32, (NB, TRUNC), 0) * BLOCK
    jj = lax.broadcasted_iota(jnp.int32, (NB, TRUNC), 1)
    widen = ((jj >= jb) & (jj < jb + BLOCK)).astype(F32)
    lanes = jnp.dot((mask[s] > 0).astype(F32), widen, preferred_element_type=F32).astype(BF)
    for b in range(NB):
        leg[s, b * BLOCK : (b + 1) * BLOCK, :] = leg[s, b * BLOCK : (b + 1) * BLOCK, :] * lanes[b : b + 1, :]


def legendre_piece(s, wavenum, low, high, spec, leg, z):
    first = KG * low // 8 * 8
    last = min(LEV, -(-KG * high // 8) * 8)
    n_rows = last - first
    degree = lax.broadcasted_iota(jnp.int32, (1, TRUNC), 1)
    upper = degree >= wavenum
    even = ((degree + wavenum) & 1) == 0
    rows = jnp.concatenate([spec[s, comp, first:last, :] for comp in range(2)], axis=0)
    rows_e = rows * jnp.where(upper & even, 1.0, 0.0).astype(BF)
    rows_o = rows * jnp.where(upper & ~even, 1.0, 0.0).astype(BF)
    both = jnp.dot(jnp.concatenate([rows_e, rows_o], axis=0), leg[s], preferred_element_type=F32)
    sums_e, sums_o = both[: 2 * n_rows], both[2 * n_rows :]
    north, south = sums_e + sums_o, sums_e - sums_o
    for comp in range(2):
        for g in range(low, high):
            n = min(KG, LEV - KG * g)
            at = n_rows * comp + KG * g - first
            dst = pl.ds(128 * g + SLOTS * comp + s, n, stride=SC)
            for t in range(TRUNC // 128):
                z[t, dst, :] = north[at : at + n, t * 128 : (t + 1) * 128]
                z[t + TRUNC // 128, dst, :] = south[at : at + n, t * 128 : (t + 1) * 128]


def round_piece(low, high, z, zb):
    part = slice(128 * low, 128 * high)
    for t in range(LT):
        zb[part, 128 * t : 128 * (t + 1)] = z[t, part, :].astype(BF)


def pack_piece(c, low, high, oht, zb, send):
    rows = lax.dot_general(
        oht[...], zb[128 * low : 128 * high, :], (((1,), (1,)), ((), ())), preferred_element_type=F32
    )
    for g in range(low, high):
        send[c, :, g] = rows[:, 128 * (g - low) : 128 * (g - low + 1)].reshape(WAVES, RW, 128).astype(BF)


def fill_order(slots, keycol, perm):
    m = columns_of(slots[...])
    half = jnp.floor(m * 0.5)
    key = TRUNC * (m - 2.0 * half) + half
    keycol[...] = jnp.full((KP, 128), -1.0, F32)
    for t in range(NT):
        n = min(TW * SLOTS, TRUNC - TW * SLOTS * t)
        part = key[TW * SLOTS * t : TW * SLOTS * t + n]
        for comp in range(2):
            keycol[128 * t + 60 * comp : 128 * t + 60 * comp + n, :] = part + float(TRUNC // 2 * comp)
    fill_onehot(perm, keycol[...], NLAT)


def fill_tables(basis, t_even, t_odd):
    n = TRUNC // 2
    t_even[:, :QUART] = basis[:TRUNC, :]
    t_odd[:, :QUART] = basis[TRUNC:, :]
    row = lax.broadcasted_iota(jnp.int32, (n, 1), 0)
    sign = jnp.where((row & 1) == 0, 1.0, -1.0).astype(F32)
    t_even[:n, QUART:] = (basis[:n, :].astype(F32) * sign).astype(BF)
    t_even[n:, QUART:] = (basis[n : 2 * n, :].astype(F32) * sign).astype(BF)
    t_odd[:n, QUART:] = (basis[3 * n :, :].astype(F32) * sign).astype(BF)
    t_odd[n:, QUART:] = (basis[2 * n : 3 * n, :].astype(F32) * -sign).astype(BF)


def fourier_piece(c, low, high, recv, regroup, lhs, perm, t_even, t_odd, quarters):
    ng = high - low
    blocks = jnp.concatenate(
        [recv[c, :, j, low:high].reshape(NT * ng * RW, 128) for j in range(TW)], axis=1
    )
    moved = jnp.dot(blocks, regroup[...], preferred_element_type=F32)
    runs = [r for r in row_runs() if low <= r[1] and r[1] < high]
    first = runs[0][3]
    last = first
    for k, start, top, at in runs:
        n = RW * (top - start)
        last = at + n
        for t in range(NT):
            src = t * ng * RW + RW * (start - low)
            lhs[at : at + n, t * 128 : (t + 1) * 128] = moved[src : src + n, k * 128 : (k + 1) * 128]
    ordered = jnp.dot(lhs[first:last, :].astype(BF), perm[...], preferred_element_type=F32).astype(BF)
    for h in range(2):
        cols = slice(h * QUART, (h + 1) * QUART)
        g_even = jnp.dot(ordered[:, :TRUNC], t_even[:, cols], preferred_element_type=F32)
        g_odd = jnp.dot(ordered[:, TRUNC:], t_odd[:, cols], preferred_element_type=F32)
        quarters[c, h, first:last, :] = (g_even + g_odd).astype(BF)
        quarters[c, h + 2, first:last, :] = (g_even - g_odd).astype(BF)
    return first, last - first


def fill_levels(levels, column, colkey, pick):
    @pl.loop(0, FIELDS * LEV)
    def _(k):
        column[pl.ds(k, 1), :] = jnp.full((1, 128), levels[k].astype(F32), F32)

    col = column[: FIELDS * LEV, :]
    for i in range(RW):
        for j in range(FIELDS * MR // 128):
            hit = col + float(1000 * i) == colkey[1:2, j * 128 : (j + 1) * 128]
            pick[FIELDS * LEV * i : FIELDS * LEV * (i + 1), j * 128 : (j + 1) * 128] = hit.astype(F32).astype(BF)


def transform_kernel(
    ws_ref, spec_ref, leg_ref, mask_ref, slots_ref, lats_ref, levels_ref, keys_ref, basis_ref, out_ref,
    spec, leg, z, zb, vcol, oht, send, recv, basis, regroup, keycol, perm, t_even, t_odd, lhs,
    quarters, xrecv, pick,
    leg_sem, load_sem, send_sem, recv_sem, xsend_sem, xrecv_sem,
):
    w, f = lax.axis_index("wave"), lax.axis_index("field")
    loads = [pltpu.make_async_copy(spec_ref, spec, load_sem.at[0]), pltpu.make_async_copy(basis_ref, basis, load_sem.at[1])]
    slot_loads = [pltpu.make_async_copy(leg_ref.at[s], leg.at[s], leg_sem.at[s]) for s in range(SLOTS)]
    loads[0].start()
    for load in slot_loads:
        load.start()
    loads[1].start()

    barrier = pltpu.get_barrier_semaphore()
    for d in range(1, FIELDS):
        pl.semaphore_signal(barrier, inc=1, device_id=(w, lax.rem(f + d, FIELDS)), device_id_type=MESH)

    lat = columns_of(lats_ref[...])
    vcol[...] = jnp.where(lat < TRUNC, lat, (NLAT + TRUNC - 1) - lat)
    clear_pads(z)

    def choose_rows(c):
        fill_onehot(oht, vcol[pl.ds(c, NLAT // CH, stride=CH), :], NLAT)

    choose_rows(0)
    loads[0].wait()

    @pl.loop(0, SLOTS // 2)
    def _(pair):
        @pl.when(pair < (WAVES - 1) // GREET)
        def _():
            for t in range(GREET):
                peer = lax.rem(w + GREET * pair + t + 1, WAVES)
                pl.semaphore_signal(barrier, inc=1, device_id=(peer, f), device_id_type=MESH)

        for half in range(2):
            s = 2 * pair + half
            pltpu.make_async_copy(leg_ref.at[s], leg.at[s], leg_sem.at[s]).wait()
        for half in range(2):
            s = 2 * pair + half
            mask_slot(s, leg, mask_ref)
            legendre_piece(s, ws_ref[SLOTS * w + s], *PIECES[0], spec, leg, z)

    my_tile, my_place = w // TW, lax.rem(w, TW)

    def wave_copy(c, p, peer):
        span = pl.ds(PIECES[p][0], PIECES[p][1] - PIECES[p][0])
        return pltpu.make_async_remote_copy(
            src_ref=send.at[c, peer, span],
            dst_ref=recv.at[c, my_tile, my_place, span],
            send_sem=send_sem,
            recv_sem=recv_sem.at[c, p],
            device_id=(peer, f),
            device_id_type=MESH,
        )

    def send_piece(c, p):
        low, high = PIECES[p]
        span = pl.ds(low, high - low)
        pack_piece(c, low, high, oht, zb, send)
        pltpu.make_async_copy(send.at[c, w, span], recv.at[c, my_tile, my_place, span], recv_sem.at[c, p]).start()

        @pl.loop(1, WAVES // 2)
        def _(d):
            wave_copy(c, p, lax.rem(w + d, WAVES)).start()
            wave_copy(c, p, lax.rem(w + WAVES - d, WAVES)).start()

        wave_copy(c, p, lax.rem(w + WAVES // 2, WAVES)).start()

    def send_chunk(c):
        choose_rows(c)
        for p in range(len(PIECES)):
            send_piece(c, p)

    round_piece(*PIECES[0], z, zb)
    pl.semaphore_wait(barrier, WAVES + FIELDS - 2)
    send_piece(0, 0)

    @pl.loop(0, SLOTS // 2)
    def _(pair):
        for half in range(2):
            s = 2 * pair + half
            legendre_piece(s, ws_ref[SLOTS * w + s], *PIECES[1], spec, leg, z)

    round_piece(*PIECES[1], z, zb)
    fill_onehot(regroup, column_of(keys_ref[0:1, :]), KG * 128)
    send_piece(0, 1)
    for c in range(CH):
        for j in range(WAVES - TW * (NT - 1), TW):
            recv[c, NT - 1, j] = jnp.zeros((NG, RW, 128), BF)
    fill_order(slots_ref, keycol, perm)
    loads[1].wait()
    fill_tables(basis, t_even, t_odd)
    send_chunk(1)
    fill_levels(levels_ref, keycol, keys_ref, pick)

    def finish_chunk(c):
        pltpu.make_async_copy(xrecv.at[c], xrecv.at[c], xrecv_sem.at[c]).wait()
        rows = xrecv[c].reshape(FIELDS * MR, QUART)
        values = jnp.dot(pick[...], rows, preferred_element_type=F32).astype(BF)
        for i in range(RW):
            out_ref[CH * i + c] = values[FIELDS * LEV * i : FIELDS * LEV * (i + 1), :]

    @pl.loop(0, CH)
    def _(c):
        for p, (low, high) in enumerate(PIECES):
            landed = send.at[c, :, pl.ds(low, high - low)]
            pltpu.make_async_copy(landed, landed, recv_sem.at[c, p]).wait()
            first, count = fourier_piece(c, low, high, recv, regroup, lhs, perm, t_even, t_odd, quarters)
            part = pl.ds(first, count)
            pltpu.make_async_copy(quarters.at[c, f, part], xrecv.at[c, f, part], xrecv_sem.at[c]).start()
            for d in (1, 3, 2):
                peer = lax.rem(f + d, FIELDS)
                pltpu.make_async_remote_copy(
                    src_ref=quarters.at[c, peer, part],
                    dst_ref=xrecv.at[c, f, part],
                    send_sem=xsend_sem,
                    recv_sem=xrecv_sem.at[c],
                    device_id=(w, peer),
                    device_id_type=MESH,
                ).start()

        @pl.when(c + 2 < CH)
        def _():
            send_chunk(c + 2)

        @pl.when(c >= 1)
        def _():
            finish_chunk(c - 1)

    finish_chunk(CH - 1)
    sent = quarters.at[:, pl.ds(0, FIELDS - 1)]
    pltpu.make_async_copy(sent, sent, xsend_sem).wait()
    left = send.at[:, pl.ds(0, WAVES - 1)]
    pltpu.make_async_copy(left, left, send_sem).wait()


def shards(spectra, legendre, block_mask, wave_slot, lat_order, level_order):
    slots = wave_slot.reshape(TRUNC // 128, 128)
    lats = lat_order.reshape(LT, 128)
    anyspace = pl.BlockSpec(memory_space=pl.ANY)
    vmem = pl.BlockSpec(memory_space=pltpu.VMEM)
    smem = pl.BlockSpec(memory_space=pltpu.SMEM)
    return pl.pallas_call(
        transform_kernel,
        out_shape=pltpu.VMEM((ROWS, FIELDS * LEV, QUART), BF),
        in_specs=[smem, anyspace, anyspace, vmem, vmem, vmem, smem, vmem, anyspace],
        out_specs=vmem,
        scratch_shapes=[
            pltpu.VMEM((SLOTS, 2, LEV, TRUNC), BF),
            pltpu.VMEM((SLOTS, TRUNC, TRUNC), BF),
            pltpu.VMEM((LT, NG * 128, 128), F32),
            pltpu.VMEM((NG * 128, NLAT), BF),
            pltpu.VMEM((NLAT, 128), F32),
            pltpu.VMEM((NLAT // CH, NLAT), BF),
            pltpu.VMEM((CH, WAVES, NG, RW, 128), BF),
            pltpu.VMEM((CH, NT, TW, NG, RW, 128), BF),
            pltpu.VMEM((2 * TRUNC, QUART), BF),
            pltpu.VMEM((TW * 128, KG * 128), BF),
            pltpu.VMEM((KP, 128), F32),
            pltpu.VMEM((KP, NLAT), BF),
            pltpu.VMEM((TRUNC, HALF), BF),
            pltpu.VMEM((TRUNC, HALF), BF),
            pltpu.VMEM((MR, KP), F32),
            pltpu.VMEM((CH, FIELDS, MR, QUART), BF),
            pltpu.VMEM((CH, FIELDS, MR, QUART), BF),
            pltpu.VMEM((RW * FIELDS * LEV, FIELDS * MR), BF),
            pltpu.SemaphoreType.DMA((SLOTS,)),
            pltpu.SemaphoreType.DMA((2,)),
            pltpu.SemaphoreType.DMA,
            pltpu.SemaphoreType.DMA((CH, len(PIECES))),
            pltpu.SemaphoreType.DMA,
            pltpu.SemaphoreType.DMA((CH,)),
        ],
        compiler_params=pltpu.CompilerParams(collective_id=0, has_side_effects=True, vmem_limit_bytes=57 << 20),
        name="transform",
    )(wave_slot, spectra, legendre, block_mask, slots, lats, level_order, jnp.asarray(key_rows()), jnp.asarray(basis_table()))


def solution(mesh):
    placed = (
        P("wave", None, "field", None),
        P("wave", None, None),
        P("wave", None, None),
        P(),
        P(),
        P(),
    )
    return jax.shard_map(
        shards, mesh=mesh, in_specs=placed, out_specs=P("wave", None, "field"), check_vma=False
    )
```

```python
import math

import jax
import jax.numpy as jnp
import numpy as np
from jax import lax
from jax.experimental import pallas as pl
from jax.experimental.pallas import tpu as pltpu
from jax.sharding import PartitionSpec as P

MESH = pl.DeviceIdType.MESH
BF = jnp.bfloat16
F32 = jnp.float32

NLON = 3072
TRUNC = 640
NLAT = 1280
BLOCK = 64
NB = 10
WAVES = 64
FIELDS = 4
SLOTS = 10
LEV = 40
ROWS = 20
HALF = NLON // 2
QUART = NLON // 4

CH = 5
RW = ROWS // CH
KG = 6
NG = 7
SC = 2 * SLOTS
TW = 6
NT = 11
KP = NT * 128
MR = RW * LEV
CUT = 3
LT = NLAT // 128
GREET = 21
PIECES = [(0, CUT), (CUT, NG)]


def row_runs():
    runs, at = [], 0
    for low, high in PIECES:
        for k in range(KG):
            top = min(high, (LEV - k + KG - 1) // KG)
            runs.append((k, low, top, at))
            at += RW * (top - low)
    return runs


def basis_table():
    q = np.arange(QUART)
    parts = []
    for odd in (0, 1):
        m = np.arange(odd, TRUNC, 2)
        ang = 2.0 * math.pi * ((m[:, None] * q[None, :]) % NLON) / NLON
        wt = np.where(m == 0, 1.0, 2.0)[:, None]
        parts += [wt * np.cos(ang), -wt * np.sin(ang)]
    return np.concatenate(parts, axis=0).astype(np.float32).astype(BF)


def key_rows():
    keys = np.full((2, TW * 128), -1.0, np.float32)
    for j in range(TW):
        for k in range(KG):
            for s in range(SC):
                keys[0, 128 * j + SC * k + s] = 128 * k + 60 * (s // SLOTS) + SLOTS * j + s % SLOTS
    for f in range(FIELDS):
        for k, low, top, at in row_runs():
            for g in range(low, top):
                for i in range(RW):
                    keys[1, MR * f + at + RW * (g - low) + i] = LEV * f + KG * g + k + 1000 * i
    return keys


def column_of(row_vec):
    return jnp.transpose(jnp.broadcast_to(row_vec, (128, row_vec.shape[1])))


def columns_of(rows):
    rows = rows.astype(F32)
    return jnp.concatenate([column_of(rows[t : t + 1, :]) for t in range(rows.shape[0])], axis=0)


def fill_onehot(ref, col, cols):
    lane = lax.broadcasted_iota(jnp.int32, col.shape, 1).astype(F32)
    for j in range(cols // 128):
        ref[:, j * 128 : (j + 1) * 128] = (col == lane + float(128 * j)).astype(F32).astype(BF)


def clear_pads(z):
    for g in range(NG):
        z[:, 128 * g + SC * KG : 128 * (g + 1), :] = jnp.zeros((LT, 128 - SC * KG, 128), F32)
    first = 128 * (NG - 1) + SC * (LEV - KG * (NG - 1))
    z[:, first : 128 * NG, :] = jnp.zeros((LT, 128 * NG - first, 128), F32)


def legendre_slot(s, wavenum, spec, leg, mask, kept, z):
    jb = lax.broadcasted_iota(jnp.int32, (NB, TRUNC), 0) * BLOCK
    jj = lax.broadcasted_iota(jnp.int32, (NB, TRUNC), 1)
    widen = ((jj >= jb) & (jj < jb + BLOCK)).astype(F32)
    lanes = jnp.dot((mask[s] > 0).astype(F32), widen, preferred_element_type=F32).astype(BF)
    for b in range(NB):
        kept[b * BLOCK : (b + 1) * BLOCK, :] = leg[s, b * BLOCK : (b + 1) * BLOCK, :] * lanes[b : b + 1, :]
    degree = lax.broadcasted_iota(jnp.int32, (1, TRUNC), 1)
    upper = degree >= wavenum
    even = ((degree + wavenum) & 1) == 0
    rows = spec[s].reshape(2 * LEV, TRUNC)
    rows_e = rows * jnp.where(upper & even, 1.0, 0.0).astype(BF)
    rows_o = rows * jnp.where(upper & ~even, 1.0, 0.0).astype(BF)
    both = jnp.dot(jnp.concatenate([rows_e, rows_o], axis=0), kept[...], preferred_element_type=F32)
    sums_e, sums_o = both[: 2 * LEV], both[2 * LEV :]
    north, south = sums_e + sums_o, sums_e - sums_o
    for comp in range(2):
        for g in range(NG):
            n = min(KG, LEV - KG * g)
            src = slice(LEV * comp + KG * g, LEV * comp + KG * g + n)
            dst = pl.ds(128 * g + SLOTS * comp + s, n, stride=SC)
            for t in range(TRUNC // 128):
                z[t, dst, :] = north[src, t * 128 : (t + 1) * 128]
                z[t + TRUNC // 128, dst, :] = south[src, t * 128 : (t + 1) * 128]


def round_piece(low, high, z, zb):
    part = slice(128 * low, 128 * high)
    for t in range(LT):
        zb[part, 128 * t : 128 * (t + 1)] = z[t, part, :].astype(BF)


def pack_piece(c, low, high, oht, zb, send):
    rows = lax.dot_general(
        oht[...], zb[128 * low : 128 * high, :], (((1,), (1,)), ((), ())), preferred_element_type=F32
    )
    for g in range(low, high):
        send[c, :, g] = rows[:, 128 * (g - low) : 128 * (g - low + 1)].reshape(WAVES, RW, 128).astype(BF)


def fill_order(slots, keycol, perm):
    m = columns_of(slots[...])
    half = jnp.floor(m * 0.5)
    key = TRUNC * (m - 2.0 * half) + half
    keycol[...] = jnp.full((KP, 128), -1.0, F32)
    for t in range(NT):
        n = min(TW * SLOTS, TRUNC - TW * SLOTS * t)
        part = key[TW * SLOTS * t : TW * SLOTS * t + n]
        for comp in range(2):
            keycol[128 * t + 60 * comp : 128 * t + 60 * comp + n, :] = part + float(TRUNC // 2 * comp)
    fill_onehot(perm, keycol[...], NLAT)


def fill_tables(basis, t_even, t_odd):
    n = TRUNC // 2
    t_even[:, :QUART] = basis[:TRUNC, :]
    t_odd[:, :QUART] = basis[TRUNC:, :]
    row = lax.broadcasted_iota(jnp.int32, (n, 1), 0)
    sign = jnp.where((row & 1) == 0, 1.0, -1.0).astype(F32)
    t_even[:n, QUART:] = (basis[:n, :].astype(F32) * sign).astype(BF)
    t_even[n:, QUART:] = (basis[n : 2 * n, :].astype(F32) * sign).astype(BF)
    t_odd[:n, QUART:] = (basis[3 * n :, :].astype(F32) * sign).astype(BF)
    t_odd[n:, QUART:] = (basis[2 * n : 3 * n, :].astype(F32) * -sign).astype(BF)


def fourier_piece(c, low, high, recv, regroup, lhs, perm, t_even, t_odd, quarters, deliver):
    ng = high - low
    blocks = jnp.concatenate(
        [recv[c, :, j, low:high].reshape(NT * ng * RW, 128) for j in range(TW)], axis=1
    )
    moved = jnp.dot(blocks, regroup[...], preferred_element_type=F32)
    runs = [r for r in row_runs() if low <= r[1] and r[1] < high]
    first = runs[0][3]
    last = first
    for k, start, top, at in runs:
        n = RW * (top - start)
        last = at + n
        for t in range(NT):
            src = t * ng * RW + RW * (start - low)
            lhs[at : at + n, t * 128 : (t + 1) * 128] = moved[src : src + n, k * 128 : (k + 1) * 128]
    ordered = jnp.dot(lhs[first:last, :].astype(BF), perm[...], preferred_element_type=F32).astype(BF)
    for h in range(2):
        cols = slice(h * QUART, (h + 1) * QUART)
        g_even = jnp.dot(ordered[:, :TRUNC], t_even[:, cols], preferred_element_type=F32)
        g_odd = jnp.dot(ordered[:, TRUNC:], t_odd[:, cols], preferred_element_type=F32)
        quarters[c, h, first:last, :] = (g_even + g_odd).astype(BF)
        quarters[c, h + 2, first:last, :] = (g_even - g_odd).astype(BF)
        for q in (h, h + 2):
            deliver(q, pl.ds(first, last - first))


def fill_levels(levels, column, colkey, pick):
    @pl.loop(0, FIELDS * LEV)
    def _(k):
        column[pl.ds(k, 1), :] = jnp.full((1, 128), levels[k].astype(F32), F32)

    col = column[: FIELDS * LEV, :]
    for i in range(RW):
        for j in range(FIELDS * MR // 128):
            hit = col + float(1000 * i) == colkey[1:2, j * 128 : (j + 1) * 128]
            pick[FIELDS * LEV * i : FIELDS * LEV * (i + 1), j * 128 : (j + 1) * 128] = hit.astype(F32).astype(BF)


def transform_kernel(
    ws_ref, spec_ref, leg_ref, mask_ref, slots_ref, lats_ref, levels_ref, keys_ref, basis_ref, out_ref,
    spec, leg, kept, z, zb, vcol, oht, send, recv, basis, regroup, keycol, perm, t_even, t_odd, lhs,
    quarters, xrecv, pick,
    leg_sem, load_sem, send_sem, recv_sem, xsend_sem, xrecv_sem,
):
    w, f = lax.axis_index("wave"), lax.axis_index("field")
    loads = [pltpu.make_async_copy(spec_ref, spec, load_sem.at[0]), pltpu.make_async_copy(basis_ref, basis, load_sem.at[1])]
    slot_loads = [pltpu.make_async_copy(leg_ref.at[s], leg.at[s], leg_sem.at[s]) for s in range(SLOTS)]
    loads[0].start()
    for load in slot_loads:
        load.start()
    loads[1].start()

    barrier = pltpu.get_barrier_semaphore()
    for d in range(1, FIELDS):
        pl.semaphore_signal(barrier, inc=1, device_id=(w, lax.rem(f + d, FIELDS)), device_id_type=MESH)

    lat = columns_of(lats_ref[...])
    vcol[...] = jnp.where(lat < TRUNC, lat, (NLAT + TRUNC - 1) - lat)
    clear_pads(z)

    def choose_rows(c):
        fill_onehot(oht, vcol[pl.ds(c, NLAT // CH, stride=CH), :], NLAT)

    choose_rows(0)
    loads[0].wait()

    @pl.loop(0, SLOTS // 2)
    def _(pair):
        @pl.when(pair < (WAVES - 1) // GREET)
        def _():
            for t in range(GREET):
                peer = lax.rem(w + GREET * pair + t + 1, WAVES)
                pl.semaphore_signal(barrier, inc=1, device_id=(peer, f), device_id_type=MESH)

        for half in range(2):
            s = 2 * pair + half
            pltpu.make_async_copy(leg_ref.at[s], leg.at[s], leg_sem.at[s]).wait()
        for half in range(2):
            s = 2 * pair + half
            legendre_slot(s, ws_ref[SLOTS * w + s], spec, leg, mask_ref, kept.at[half], z)

    my_tile, my_place = w // TW, lax.rem(w, TW)

    def wave_copy(c, p, peer):
        span = pl.ds(PIECES[p][0], PIECES[p][1] - PIECES[p][0])
        return pltpu.make_async_remote_copy(
            src_ref=send.at[c, peer, span],
            dst_ref=recv.at[c, my_tile, my_place, span],
            send_sem=send_sem,
            recv_sem=recv_sem.at[c, p],
            device_id=(peer, f),
            device_id_type=MESH,
        )

    def send_piece(c, p):
        low, high = PIECES[p]
        span = pl.ds(low, high - low)
        pack_piece(c, low, high, oht, zb, send)
        pltpu.make_async_copy(send.at[c, w, span], recv.at[c, my_tile, my_place, span], recv_sem.at[c, p]).start()

        @pl.loop(1, WAVES // 2)
        def _(d):
            wave_copy(c, p, lax.rem(w + d, WAVES)).start()
            wave_copy(c, p, lax.rem(w + WAVES - d, WAVES)).start()

        wave_copy(c, p, lax.rem(w + WAVES // 2, WAVES)).start()

    def send_chunk(c):
        choose_rows(c)
        for p in range(len(PIECES)):
            send_piece(c, p)

    round_piece(*PIECES[0], z, zb)
    pl.semaphore_wait(barrier, WAVES + FIELDS - 2)
    send_piece(0, 0)
    round_piece(*PIECES[1], z, zb)
    fill_onehot(regroup, column_of(keys_ref[0:1, :]), KG * 128)
    send_piece(0, 1)
    for c in range(CH):
        for j in range(WAVES - TW * (NT - 1), TW):
            recv[c, NT - 1, j] = jnp.zeros((NG, RW, 128), BF)
    fill_order(slots_ref, keycol, perm)
    loads[1].wait()
    fill_tables(basis, t_even, t_odd)

    def finish_chunk(c):
        pltpu.make_async_copy(xrecv.at[c], xrecv.at[c], xrecv_sem.at[c]).wait()
        rows = xrecv[c].reshape(FIELDS * MR, QUART)
        values = jnp.dot(pick[...], rows, preferred_element_type=F32).astype(BF)
        for i in range(RW):
            out_ref[CH * i + c] = values[FIELDS * LEV * i : FIELDS * LEV * (i + 1), :]

    @pl.loop(0, CH)
    def _(c):
        def deliver(q, part):
            @pl.when(f == q)
            def _():
                pltpu.make_async_copy(quarters.at[c, q, part], xrecv.at[c, q, part], xrecv_sem.at[c]).start()

            @pl.when(f != q)
            def _():
                pltpu.make_async_remote_copy(
                    src_ref=quarters.at[c, q, part],
                    dst_ref=xrecv.at[c, f, part],
                    send_sem=xsend_sem,
                    recv_sem=xrecv_sem.at[c],
                    device_id=(w, q),
                    device_id_type=MESH,
                ).start()

        for p, (low, high) in enumerate(PIECES):
            landed = send.at[c, :, pl.ds(low, high - low)]
            pltpu.make_async_copy(landed, landed, recv_sem.at[c, p]).wait()
            fourier_piece(c, low, high, recv, regroup, lhs, perm, t_even, t_odd, quarters, deliver)
            if p == 0:

                @pl.when(c == 0)
                def _():
                    send_chunk(1)

        @pl.when(c + 2 < CH)
        def _():
            send_chunk(c + 2)

        @pl.when(c == 0)
        def _():
            fill_levels(levels_ref, keycol, keys_ref, pick)

        @pl.when(c >= 1)
        def _():
            finish_chunk(c - 1)

    finish_chunk(CH - 1)
    sent = quarters.at[:, pl.ds(0, FIELDS - 1)]
    pltpu.make_async_copy(sent, sent, xsend_sem).wait()
    left = send.at[:, pl.ds(0, WAVES - 1)]
    pltpu.make_async_copy(left, left, send_sem).wait()


def shards(spectra, legendre, block_mask, wave_slot, lat_order, level_order):
    slots = wave_slot.reshape(TRUNC // 128, 128)
    lats = lat_order.reshape(LT, 128)
    anyspace = pl.BlockSpec(memory_space=pl.ANY)
    vmem = pl.BlockSpec(memory_space=pltpu.VMEM)
    smem = pl.BlockSpec(memory_space=pltpu.SMEM)
    return pl.pallas_call(
        transform_kernel,
        out_shape=pltpu.VMEM((ROWS, FIELDS * LEV, QUART), BF),
        in_specs=[smem, anyspace, anyspace, vmem, vmem, vmem, smem, vmem, anyspace],
        out_specs=vmem,
        scratch_shapes=[
            pltpu.VMEM((SLOTS, 2, LEV, TRUNC), BF),
            pltpu.VMEM((SLOTS, TRUNC, TRUNC), BF),
            pltpu.VMEM((2, TRUNC, TRUNC), BF),
            pltpu.VMEM((LT, NG * 128, 128), F32),
            pltpu.VMEM((NG * 128, NLAT), BF),
            pltpu.VMEM((NLAT, 128), F32),
            pltpu.VMEM((NLAT // CH, NLAT), BF),
            pltpu.VMEM((CH, WAVES, NG, RW, 128), BF),
            pltpu.VMEM((CH, NT, TW, NG, RW, 128), BF),
            pltpu.VMEM((2 * TRUNC, QUART), BF),
            pltpu.VMEM((TW * 128, KG * 128), BF),
            pltpu.VMEM((KP, 128), F32),
            pltpu.VMEM((KP, NLAT), BF),
            pltpu.VMEM((TRUNC, HALF), BF),
            pltpu.VMEM((TRUNC, HALF), BF),
            pltpu.VMEM((MR, KP), F32),
            pltpu.VMEM((CH, FIELDS, MR, QUART), BF),
            pltpu.VMEM((CH, FIELDS, MR, QUART), BF),
            pltpu.VMEM((RW * FIELDS * LEV, FIELDS * MR), BF),
            pltpu.SemaphoreType.DMA((SLOTS,)),
            pltpu.SemaphoreType.DMA((2,)),
            pltpu.SemaphoreType.DMA,
            pltpu.SemaphoreType.DMA((CH, len(PIECES))),
            pltpu.SemaphoreType.DMA,
            pltpu.SemaphoreType.DMA((CH,)),
        ],
        compiler_params=pltpu.CompilerParams(collective_id=0, has_side_effects=True, vmem_limit_bytes=57 << 20),
        name="transform",
    )(wave_slot, spectra, legendre, block_mask, slots, lats, level_order, jnp.asarray(key_rows()), jnp.asarray(basis_table()))


def solution(mesh):
    placed = (
        P("wave", None, "field", None),
        P("wave", None, None),
        P("wave", None, None),
        P(),
        P(),
        P(),
    )
    return jax.shard_map(
        shards, mesh=mesh, in_specs=placed, out_specs=P("wave", None, "field"), check_vma=False
    )
```

```python
import math

import jax
import jax.numpy as jnp
import numpy as np
from jax import lax
from jax.experimental import pallas as pl
from jax.experimental.pallas import tpu as pltpu
from jax.sharding import PartitionSpec as P

MESH = pl.DeviceIdType.MESH
BF = jnp.bfloat16
F32 = jnp.float32

NLON = 3072
TRUNC = 640
NLAT = 1280
BLOCK = 64
NB = 10
WAVES = 64
FIELDS = 4
SLOTS = 10
LEV = 40
ROWS = 20
HALF = NLON // 2
QUART = NLON // 4

CH = 5
RW = ROWS // CH
KG = 6
NG = 7
SC = 2 * SLOTS
TW = 6
NT = 11
KP = NT * 128
MR = RW * LEV
CUT = 3
LT = NLAT // 128
GREET = 21
PIECES = [(0, CUT), (CUT, NG)]


def row_runs():
    runs, at = [], 0
    for low, high in PIECES:
        for k in range(KG):
            top = min(high, (LEV - k + KG - 1) // KG)
            runs.append((k, low, top, at))
            at += RW * (top - low)
    return runs


def basis_table():
    q = np.arange(QUART)
    parts = []
    for odd in (0, 1):
        m = np.arange(odd, TRUNC, 2)
        ang = 2.0 * math.pi * ((m[:, None] * q[None, :]) % NLON) / NLON
        wt = np.where(m == 0, 1.0, 2.0)[:, None]
        parts += [wt * np.cos(ang), -wt * np.sin(ang)]
    return np.concatenate(parts, axis=0).astype(np.float32).astype(BF)


def key_rows():
    keys = np.full((2, TW * 128), -1.0, np.float32)
    for j in range(TW):
        for k in range(KG):
            for s in range(SC):
                keys[0, 128 * j + SC * k + s] = 128 * k + 60 * (s // SLOTS) + SLOTS * j + s % SLOTS
    for f in range(FIELDS):
        for k, low, top, at in row_runs():
            for g in range(low, top):
                for i in range(RW):
                    keys[1, MR * f + at + RW * (g - low) + i] = LEV * f + KG * g + k + 1000 * i
    return keys


def column_of(row_vec):
    return jnp.transpose(jnp.broadcast_to(row_vec, (128, row_vec.shape[1])))


def columns_of(rows):
    rows = rows.astype(F32)
    return jnp.concatenate([column_of(rows[t : t + 1, :]) for t in range(rows.shape[0])], axis=0)


def fill_onehot(ref, col, cols):
    lane = lax.broadcasted_iota(jnp.int32, col.shape, 1).astype(F32)
    for j in range(cols // 128):
        ref[:, j * 128 : (j + 1) * 128] = (col == lane + float(128 * j)).astype(F32).astype(BF)


def clear_pads(z):
    for g in range(NG):
        z[:, 128 * g + SC * KG : 128 * (g + 1), :] = jnp.zeros((LT, 128 - SC * KG, 128), F32)
    first = 128 * (NG - 1) + SC * (LEV - KG * (NG - 1))
    z[:, first : 128 * NG, :] = jnp.zeros((LT, 128 * NG - first, 128), F32)


def legendre_slot(s, wavenum, spec, leg, mask, kept, z):
    jb = lax.broadcasted_iota(jnp.int32, (NB, TRUNC), 0) * BLOCK
    jj = lax.broadcasted_iota(jnp.int32, (NB, TRUNC), 1)
    widen = ((jj >= jb) & (jj < jb + BLOCK)).astype(F32)
    lanes = jnp.dot((mask[s] > 0).astype(F32), widen, preferred_element_type=F32).astype(BF)
    for b in range(NB):
        kept[b * BLOCK : (b + 1) * BLOCK, :] = leg[s, b * BLOCK : (b + 1) * BLOCK, :] * lanes[b : b + 1, :]
    degree = lax.broadcasted_iota(jnp.int32, (1, TRUNC), 1)
    upper = degree >= wavenum
    even = ((degree + wavenum) & 1) == 0
    rows = spec[s].reshape(2 * LEV, TRUNC)
    rows_e = rows * jnp.where(upper & even, 1.0, 0.0).astype(BF)
    rows_o = rows * jnp.where(upper & ~even, 1.0, 0.0).astype(BF)
    both = jnp.dot(jnp.concatenate([rows_e, rows_o], axis=0), kept[...], preferred_element_type=F32)
    sums_e, sums_o = both[: 2 * LEV], both[2 * LEV :]
    north, south = sums_e + sums_o, sums_e - sums_o
    for comp in range(2):
        for g in range(NG):
            n = min(KG, LEV - KG * g)
            src = slice(LEV * comp + KG * g, LEV * comp + KG * g + n)
            dst = pl.ds(128 * g + SLOTS * comp + s, n, stride=SC)
            for t in range(TRUNC // 128):
                z[t, dst, :] = north[src, t * 128 : (t + 1) * 128]
                z[t + TRUNC // 128, dst, :] = south[src, t * 128 : (t + 1) * 128]


def round_piece(low, high, z, zb):
    part = slice(128 * low, 128 * high)
    for t in range(LT):
        zb[part, 128 * t : 128 * (t + 1)] = z[t, part, :].astype(BF)


def pack_piece(c, low, high, oht, zb, send):
    rows = lax.dot_general(
        oht[...], zb[128 * low : 128 * high, :], (((1,), (1,)), ((), ())), preferred_element_type=F32
    )
    for g in range(low, high):
        send[c, :, g] = rows[:, 128 * (g - low) : 128 * (g - low + 1)].reshape(WAVES, RW, 128).astype(BF)


def fill_order(slots, keycol, perm):
    m = columns_of(slots[...])
    half = jnp.floor(m * 0.5)
    key = TRUNC * (m - 2.0 * half) + half
    keycol[...] = jnp.full((KP, 128), -1.0, F32)
    for t in range(NT):
        n = min(TW * SLOTS, TRUNC - TW * SLOTS * t)
        part = key[TW * SLOTS * t : TW * SLOTS * t + n]
        for comp in range(2):
            keycol[128 * t + 60 * comp : 128 * t + 60 * comp + n, :] = part + float(TRUNC // 2 * comp)
    fill_onehot(perm, keycol[...], NLAT)


def fill_tables(basis, t_even, t_odd):
    n = TRUNC // 2
    t_even[:, :QUART] = basis[:TRUNC, :]
    t_odd[:, :QUART] = basis[TRUNC:, :]
    row = lax.broadcasted_iota(jnp.int32, (n, 1), 0)
    sign = jnp.where((row & 1) == 0, 1.0, -1.0).astype(F32)
    t_even[:n, QUART:] = (basis[:n, :].astype(F32) * sign).astype(BF)
    t_even[n:, QUART:] = (basis[n : 2 * n, :].astype(F32) * sign).astype(BF)
    t_odd[:n, QUART:] = (basis[3 * n :, :].astype(F32) * sign).astype(BF)
    t_odd[n:, QUART:] = (basis[2 * n : 3 * n, :].astype(F32) * -sign).astype(BF)


def fourier_piece(c, low, high, recv, regroup, lhs, perm, t_even, t_odd, quarters):
    ng = high - low
    blocks = jnp.concatenate(
        [recv[c, :, j, low:high].reshape(NT * ng * RW, 128) for j in range(TW)], axis=1
    )
    moved = jnp.dot(blocks, regroup[...], preferred_element_type=F32)
    runs = [r for r in row_runs() if low <= r[1] and r[1] < high]
    first = runs[0][3]
    last = first
    for k, start, top, at in runs:
        n = RW * (top - start)
        last = at + n
        for t in range(NT):
            src = t * ng * RW + RW * (start - low)
            lhs[at : at + n, t * 128 : (t + 1) * 128] = moved[src : src + n, k * 128 : (k + 1) * 128]
    ordered = jnp.dot(lhs[first:last, :].astype(BF), perm[...], preferred_element_type=F32).astype(BF)
    for h in range(2):
        cols = slice(h * QUART, (h + 1) * QUART)
        g_even = jnp.dot(ordered[:, :TRUNC], t_even[:, cols], preferred_element_type=F32)
        g_odd = jnp.dot(ordered[:, TRUNC:], t_odd[:, cols], preferred_element_type=F32)
        quarters[c, h, first:last, :] = (g_even + g_odd).astype(BF)
        quarters[c, h + 2, first:last, :] = (g_even - g_odd).astype(BF)
    return first, last - first


def fill_levels(levels, column, colkey, pick):
    @pl.loop(0, FIELDS * LEV)
    def _(k):
        column[pl.ds(k, 1), :] = jnp.full((1, 128), levels[k].astype(F32), F32)

    col = column[: FIELDS * LEV, :]
    for i in range(RW):
        for j in range(FIELDS * MR // 128):
            hit = col + float(1000 * i) == colkey[1:2, j * 128 : (j + 1) * 128]
            pick[FIELDS * LEV * i : FIELDS * LEV * (i + 1), j * 128 : (j + 1) * 128] = hit.astype(F32).astype(BF)


def transform_kernel(
    ws_ref, spec_ref, leg_ref, mask_ref, slots_ref, lats_ref, levels_ref, keys_ref, basis_ref, out_ref,
    spec, leg, kept, z, zb, vcol, oht, send, recv, basis, regroup, keycol, perm, t_even, t_odd, lhs,
    quarters, xrecv, pick,
    leg_sem, load_sem, send_sem, recv_sem, xsend_sem, xrecv_sem,
):
    w, f = lax.axis_index("wave"), lax.axis_index("field")
    loads = [pltpu.make_async_copy(spec_ref, spec, load_sem.at[0]), pltpu.make_async_copy(basis_ref, basis, load_sem.at[1])]
    slot_loads = [pltpu.make_async_copy(leg_ref.at[s], leg.at[s], leg_sem.at[s]) for s in range(SLOTS)]
    loads[0].start()
    for load in slot_loads:
        load.start()
    loads[1].start()

    barrier = pltpu.get_barrier_semaphore()
    for d in range(1, FIELDS):
        pl.semaphore_signal(barrier, inc=1, device_id=(w, lax.rem(f + d, FIELDS)), device_id_type=MESH)

    lat = columns_of(lats_ref[...])
    vcol[...] = jnp.where(lat < TRUNC, lat, (NLAT + TRUNC - 1) - lat)
    clear_pads(z)

    def choose_rows(c):
        fill_onehot(oht, vcol[pl.ds(c, NLAT // CH, stride=CH), :], NLAT)

    choose_rows(0)
    loads[0].wait()

    @pl.loop(0, SLOTS // 2)
    def _(pair):
        @pl.when(pair < (WAVES - 1) // GREET)
        def _():
            for t in range(GREET):
                peer = lax.rem(w + GREET * pair + t + 1, WAVES)
                pl.semaphore_signal(barrier, inc=1, device_id=(peer, f), device_id_type=MESH)

        for half in range(2):
            s = 2 * pair + half
            pltpu.make_async_copy(leg_ref.at[s], leg.at[s], leg_sem.at[s]).wait()
        for half in range(2):
            s = 2 * pair + half
            legendre_slot(s, ws_ref[SLOTS * w + s], spec, leg, mask_ref, kept.at[half], z)

    my_tile, my_place = w // TW, lax.rem(w, TW)

    def wave_copy(c, p, peer):
        span = pl.ds(PIECES[p][0], PIECES[p][1] - PIECES[p][0])
        return pltpu.make_async_remote_copy(
            src_ref=send.at[c, peer, span],
            dst_ref=recv.at[c, my_tile, my_place, span],
            send_sem=send_sem,
            recv_sem=recv_sem.at[c, p],
            device_id=(peer, f),
            device_id_type=MESH,
        )

    def send_piece(c, p):
        low, high = PIECES[p]
        span = pl.ds(low, high - low)
        pack_piece(c, low, high, oht, zb, send)
        pltpu.make_async_copy(send.at[c, w, span], recv.at[c, my_tile, my_place, span], recv_sem.at[c, p]).start()

        @pl.loop(1, WAVES // 2)
        def _(d):
            wave_copy(c, p, lax.rem(w + d, WAVES)).start()
            wave_copy(c, p, lax.rem(w + WAVES - d, WAVES)).start()

        wave_copy(c, p, lax.rem(w + WAVES // 2, WAVES)).start()

    def send_chunk(c):
        choose_rows(c)
        for p in range(len(PIECES)):
            send_piece(c, p)

    round_piece(*PIECES[0], z, zb)
    pl.semaphore_wait(barrier, WAVES + FIELDS - 2)
    send_piece(0, 0)
    round_piece(*PIECES[1], z, zb)
    fill_onehot(regroup, column_of(keys_ref[0:1, :]), KG * 128)
    send_piece(0, 1)
    for c in range(CH):
        for j in range(WAVES - TW * (NT - 1), TW):
            recv[c, NT - 1, j] = jnp.zeros((NG, RW, 128), BF)
    fill_order(slots_ref, keycol, perm)
    loads[1].wait()
    fill_tables(basis, t_even, t_odd)
    send_chunk(1)

    def finish_chunk(c):
        pltpu.make_async_copy(xrecv.at[c], xrecv.at[c], xrecv_sem.at[c]).wait()
        rows = xrecv[c].reshape(FIELDS * MR, QUART)
        values = jnp.dot(pick[...], rows, preferred_element_type=F32).astype(BF)
        for i in range(RW):
            out_ref[CH * i + c] = values[FIELDS * LEV * i : FIELDS * LEV * (i + 1), :]

    @pl.loop(0, CH)
    def _(c):
        for p, (low, high) in enumerate(PIECES):
            landed = send.at[c, :, pl.ds(low, high - low)]
            pltpu.make_async_copy(landed, landed, recv_sem.at[c, p]).wait()
            first, count = fourier_piece(c, low, high, recv, regroup, lhs, perm, t_even, t_odd, quarters)
            part = pl.ds(first, count)
            pltpu.make_async_copy(quarters.at[c, f, part], xrecv.at[c, f, part], xrecv_sem.at[c]).start()
            for d in (1, 3, 2):
                peer = lax.rem(f + d, FIELDS)
                pltpu.make_async_remote_copy(
                    src_ref=quarters.at[c, peer, part],
                    dst_ref=xrecv.at[c, f, part],
                    send_sem=xsend_sem,
                    recv_sem=xrecv_sem.at[c],
                    device_id=(w, peer),
                    device_id_type=MESH,
                ).start()

        @pl.when(c + 2 < CH)
        def _():
            send_chunk(c + 2)

        @pl.when(c == 0)
        def _():
            fill_levels(levels_ref, keycol, keys_ref, pick)

        @pl.when(c >= 1)
        def _():
            finish_chunk(c - 1)

    finish_chunk(CH - 1)
    sent = quarters.at[:, pl.ds(0, FIELDS - 1)]
    pltpu.make_async_copy(sent, sent, xsend_sem).wait()
    left = send.at[:, pl.ds(0, WAVES - 1)]
    pltpu.make_async_copy(left, left, send_sem).wait()


def shards(spectra, legendre, block_mask, wave_slot, lat_order, level_order):
    slots = wave_slot.reshape(TRUNC // 128, 128)
    lats = lat_order.reshape(LT, 128)
    anyspace = pl.BlockSpec(memory_space=pl.ANY)
    vmem = pl.BlockSpec(memory_space=pltpu.VMEM)
    smem = pl.BlockSpec(memory_space=pltpu.SMEM)
    return pl.pallas_call(
        transform_kernel,
        out_shape=pltpu.VMEM((ROWS, FIELDS * LEV, QUART), BF),
        in_specs=[smem, anyspace, anyspace, vmem, vmem, vmem, smem, vmem, anyspace],
        out_specs=vmem,
        scratch_shapes=[
            pltpu.VMEM((SLOTS, 2, LEV, TRUNC), BF),
            pltpu.VMEM((SLOTS, TRUNC, TRUNC), BF),
            pltpu.VMEM((2, TRUNC, TRUNC), BF),
            pltpu.VMEM((LT, NG * 128, 128), F32),
            pltpu.VMEM((NG * 128, NLAT), BF),
            pltpu.VMEM((NLAT, 128), F32),
            pltpu.VMEM((NLAT // CH, NLAT), BF),
            pltpu.VMEM((CH, WAVES, NG, RW, 128), BF),
            pltpu.VMEM((CH, NT, TW, NG, RW, 128), BF),
            pltpu.VMEM((2 * TRUNC, QUART), BF),
            pltpu.VMEM((TW * 128, KG * 128), BF),
            pltpu.VMEM((KP, 128), F32),
            pltpu.VMEM((KP, NLAT), BF),
            pltpu.VMEM((TRUNC, HALF), BF),
            pltpu.VMEM((TRUNC, HALF), BF),
            pltpu.VMEM((MR, KP), F32),
            pltpu.VMEM((CH, FIELDS, MR, QUART), BF),
            pltpu.VMEM((CH, FIELDS, MR, QUART), BF),
            pltpu.VMEM((RW * FIELDS * LEV, FIELDS * MR), BF),
            pltpu.SemaphoreType.DMA((SLOTS,)),
            pltpu.SemaphoreType.DMA((2,)),
            pltpu.SemaphoreType.DMA,
            pltpu.SemaphoreType.DMA((CH, len(PIECES))),
            pltpu.SemaphoreType.DMA,
            pltpu.SemaphoreType.DMA((CH,)),
        ],
        compiler_params=pltpu.CompilerParams(collective_id=0, has_side_effects=True, vmem_limit_bytes=57 << 20),
        name="transform",
    )(wave_slot, spectra, legendre, block_mask, slots, lats, level_order, jnp.asarray(key_rows()), jnp.asarray(basis_table()))


def solution(mesh):
    placed = (
        P("wave", None, "field", None),
        P("wave", None, None),
        P("wave", None, None),
        P(),
        P(),
        P(),
    )
    return jax.shard_map(
        shards, mesh=mesh, in_specs=placed, out_specs=P("wave", None, "field"), check_vma=False
    )
```
